32 devices in a mesh: groups: 2 (over x), seq: 8 (over z, y), head: 2 (over core).
Axes of the slice: x: 2, y: 2, z: 4, core: 2. Of those that a mesh axis runs over, the one named last changes fastest.
Arguments:
- query_rows: bfloat16 [2048, 6144], P(('groups', 'seq'), 'head'), parts along dimension 0
- key_rows: bfloat16 [2048, 6144], P(('groups', 'seq'), 'head'), parts along dimension 0, may hold values from -6 to 6
- value_rows: bfloat16 [2048, 6144], P(('groups', 'seq'), 'head'), parts along dimension 0, may hold values from -6 to 6
- key_len: int32 [16], P('groups'), parts along dimension 0, may hold values from 2 to 128, as said below
- linear_scale: float32 [48], P('head'), may hold values from 0.5 to 2
Outputs:
- attended: bfloat16 [2048, 6144], P(('groups', 'seq'), 'head'), parts along dimension 0
The draws below stay inside these ranges and needn't reach their ends.
There are 2 independent parts, one for each index of `groups`. The reference program is written for one: setup_inputs(seed, part) draws one part's arguments, and reference() takes and returns one part's arrays. A program takes and returns all parts, laid end to end along the dimension named above; an argument that names none is the same for every part. Nothing has to cross between parts.
Inputs may be any that keep to these rules, and one draw needn't show every extreme that they name: `key_len`: one block has exactly 128 valid keys in every draw.
All inputs are finite; a program needn't handle non-finite values.
Results may differ from the reference program's by a relative error of at most 0.00135.
Values may be sent and summed in bfloat16 or wider, within the bound.
A program may use at most 256 MiB of HBM per device.

```python
import math
import jax
import jax.numpy as jnp
from jax import lax

HD = 128
HEADS = 48
BLOCK = 128
TOKENS = 1024


def base_keys(key):
    source = jax.random.fold_in(key, 11)
    drawn = jax.random.truncated_normal(source, -6.0, 6.0, (TOKENS, HEADS * HD), jnp.float32)
    return drawn


def draw_key_rows(key, part):
    return base_keys(key).astype(jnp.bfloat16)


def draw_query_rows(key, part):
    source = jax.random.fold_in(key, 12)
    drawn = 3.0 * jax.random.truncated_normal(source, -6.0, 6.0, (TOKENS, HEADS * HD), jnp.float32)
    return drawn.astype(jnp.bfloat16)


def draw_key_len(key, part):
    block_count = TOKENS // BLOCK
    lengths = jax.random.randint(jax.random.fold_in(key, 21), (block_count,), 2, BLOCK + 1, dtype=jnp.int32)
    chosen = jax.random.randint(jax.random.fold_in(key, 22), (), 0, block_count, dtype=jnp.int32)
    return lengths.at[chosen].set(BLOCK)


def steps_of(own_key, extent, cuts, least, high):
    gain, own = 1.0, jax.random.fold_in(own_key, 6)
    for dim, blocks in cuts:
        heights = jnp.exp(jax.random.uniform(jax.random.fold_in(own, dim), (blocks,), jnp.float32, least / len(cuts), high / len(cuts)))
        gain = gain * jnp.repeat(heights, extent[dim] // blocks).reshape([-1 if axis == dim else 1 for axis in range(len(extent))])
    return gain


def noise(own_key, dims, width, most, cuts=(), kind=jnp.bfloat16):
    loudness = steps_of(own_key, dims, cuts, -0.22, 0.18) if cuts else 1.0
    array = jax.random.normal(own_key, dims, jnp.float32) * width * loudness
    return jnp.minimum(jnp.maximum(array, -most), most).astype(kind)


def setup_inputs(seed: int = 0, part: int = 0) -> dict:
    key_list = jax.random.split(jax.random.key(seed), 6)
    part_keys = jax.random.split(jax.random.fold_in(key_list[5], part), 6)
    return {
        "query_rows": draw_query_rows(jax.random.fold_in(jax.random.fold_in(key_list[5], part), 71), part),
        "key_rows": draw_key_rows(jax.random.fold_in(jax.random.fold_in(key_list[5], part), 71), part),
        "value_rows": noise(part_keys[2], (TOKENS, HEADS * HD), 1.0, 6.0, ((0, 8), (1, 2))),
        "key_len": draw_key_len(jax.random.fold_in(jax.random.fold_in(key_list[5], part), 71), part),
        "linear_scale": jnp.clip(jnp.exp(math.log(2.0) - 1.3862944 * jax.random.uniform(key_list[4], (HEADS,), jnp.float32) ** steps_of(key_list[4], (HEADS,), ((0, 2),), -0.2, 0.2)), 0.5, 2.0),
    }


def feature(inputs):
    return jnp.where(inputs > 0.0, inputs + 1.0, jnp.exp(jnp.minimum(inputs, 0.0)))

def partial_block(query_block, key_block, value_block, live_count, causal):
    scores = jnp.einsum('rhd,chd->hrc', query_block.astype(jnp.float32), key_block.astype(jnp.float32), precision=lax.Precision.HIGHEST) * (1.0 / math.sqrt(HD))
    columns = lax.broadcasted_iota(jnp.int32, scores.shape, 2)
    allowed = columns < live_count
    if causal:
        allowed = allowed & (columns <= lax.broadcasted_iota(jnp.int32, scores.shape, 1))
    row_peak = lax.optimization_barrier(jnp.max(jnp.where(allowed, scores, -jnp.inf), axis=2))
    weights = jnp.where(allowed, jnp.exp(scores - row_peak[:, :, None]), 0.0).astype(jnp.bfloat16)
    row_total = lax.optimization_barrier(jnp.sum(weights.astype(jnp.float32), axis=2))
    numerator = jnp.einsum('hrc,chd->rhd', weights.astype(jnp.float32), value_block.astype(jnp.float32), precision=lax.Precision.HIGHEST)
    return (numerator, row_peak, row_total)

def combine(pieces):
    row_peak = pieces[0][1]
    for one_piece in pieces[1:]:
        row_peak = jnp.maximum(row_peak, one_piece[1])
    numerator = jnp.zeros_like(pieces[0][0])
    denominator = jnp.zeros_like(pieces[0][2])
    for one_piece in pieces:
        factor = jnp.exp(one_piece[1] - row_peak)
        numerator = numerator + jnp.transpose(factor)[:, :, None] * one_piece[0]
        denominator = denominator + factor * one_piece[2]
    return numerator / jnp.transpose(denominator)[:, :, None]

def reference(query_rows, key_rows, value_rows, key_len, linear_scale):
    blocks = TOKENS // BLOCK
    levels = blocks.bit_length() - 1
    queries = query_rows.reshape(blocks, BLOCK, HEADS, HD)
    key_heads = key_rows.reshape(blocks, BLOCK, HEADS, HD)
    value_heads = value_rows.reshape(blocks, BLOCK, HEADS, HD)

    def block_sum(inputs):
        key_block, value_block, live_count = inputs
        live_rows = (jnp.arange(BLOCK, dtype=jnp.int32) < live_count)[:, None, None]
        mapped = jnp.where(live_rows, feature(key_block.astype(jnp.float32)), 0.0)
        return jnp.einsum('rhd,rhe->hde', mapped, value_block.astype(jnp.float32), precision=lax.Precision.HIGHEST)
    all_sums = lax.map(block_sum, (key_heads, value_heads, key_len))
    prefix = jnp.concatenate([jnp.zeros_like(all_sums[:1]), jnp.cumsum(all_sums[:-1], axis=0)], axis=0)

    def one_block(inputs):
        query_block, prefix_block, block_id = inputs
        pieces = [partial_block(query_block, key_heads[block_id], value_heads[block_id], key_len[block_id], True)]
        for bit_level in range(levels):
            partner = jnp.bitwise_xor(block_id, 1 << bit_level).astype(jnp.int32)
            pieces.append(partial_block(query_block, key_heads[partner], value_heads[partner], key_len[partner], False))
        attention = combine(pieces)
        linear = jnp.einsum('rhd,hde->rhe', feature(query_block.astype(jnp.float32)), prefix_block, precision=lax.Precision.HIGHEST)
        linear = linear * (linear_scale[None, :, None] / (HD * math.sqrt(TOKENS)))
        return (attention + linear).astype(jnp.bfloat16)
    output = lax.map(one_block, (queries, prefix, jnp.arange(blocks, dtype=jnp.int32)))
    return output.reshape(TOKENS, HEADS * HD)
```

```python
import functools
import math

import jax
import jax.numpy as jnp
from jax import lax
from jax.experimental import pallas as pl
from jax.experimental.pallas import tpu as pltpu
from jax.sharding import PartitionSpec as P

HEADS_PER_CHUNK = 2
WINDOW = 3
LAG_TIMES = 5
LAG_OVER = 3


def feature(inputs):
    return jnp.where(inputs > 0.0, inputs + 1.0, jnp.exp(jnp.minimum(inputs, 0.0)))


def two_terms(wide):
    coarse = wide.astype(jnp.bfloat16)
    return coarse, (wide - coarse.astype(jnp.float32)).astype(jnp.bfloat16)


def kernel(
    blocks, heads, width, per_chunk, window, delay, serve,
    len_hbm, scale_hbm, q_hbm, k_hbm, v_hbm, out_ref,
    len_ref, scale_ref, q_ref, k_ref, v_ref, load_sem, far, acc, own_sums, near_sums, chain_out, chain_in, swap_in,
    send_sem, recv_sem, chain_send, chain_recv, swap_send, swap_recv,
    guest_q, served_out, served_in, stats_out, stats_in, ask_send, ask_recv, answer_send, answer_recv,
):
    rows = q_ref.shape[0]
    levels = blocks.bit_length() - 1
    chunks = heads // per_chunk
    half = chunks // 2
    pairs = blocks // 2
    span = per_chunk * width
    linear_lag = max(half, delay(pairs - 1) + 1)
    linear_first = linear_lag == half
    turns = max(chunks, half + linear_lag)

    me = lax.axis_index("seq")
    side = lax.rem(me, 2)
    pair = me // 2
    partners = [me + (1 - 2 * lax.rem(me // (1 << bit), 2)) * (1 << bit) for bit in range(levels)]
    above = lax.rem(me + 2, blocks)
    below = lax.rem(me + blocks - 2, blocks)

    def place(turn, which):
        return lax.rem(turn + half * which, chunks)

    def columns(chunk):
        return pl.ds(pl.multiple_of(chunk * span, span), span)

    def block_copy(bit, turn, part, which):
        source = k_hbm if part == 0 else v_hbm
        cut = columns(place(turn, which))
        return pltpu.make_async_remote_copy(
            src_ref=source.at[:, cut],
            dst_ref=far.at[bit, part, :, cut],
            send_sem=send_sem.at[bit, turn, part],
            recv_sem=recv_sem.at[bit, turn, part],
            device_id={"seq": partners[bit] if isinstance(bit, int) else partners[1]},
            device_id_type=pl.DeviceIdType.MESH,
        )

    def chain_copy(turn):
        return pltpu.make_async_remote_copy(
            src_ref=chain_out.at[turn],
            dst_ref=chain_in.at[turn],
            send_sem=chain_send.at[turn],
            recv_sem=chain_recv.at[turn],
            device_id={"seq": above},
            device_id_type=pl.DeviceIdType.MESH,
        )

    def swap_copy(turn):
        return pltpu.make_async_remote_copy(
            src_ref=chain_in.at[turn],
            dst_ref=swap_in.at[turn],
            send_sem=swap_send.at[turn],
            recv_sem=swap_recv.at[turn],
            device_id={"seq": partners[0]},
            device_id_type=pl.DeviceIdType.MESH,
        )

    host = jnp.where(pair == 1, below, partners[-1])
    guest = jnp.where(pair == 0, above, partners[-1])

    def served(turn):
        return (turn >= half) & (lax.rem(turn, 2) == 1) if serve else False

    def served_turn(index):
        return half + 1 - half % 2 + 2 * index

    def served_index(turn):
        return (turn - half) // 2

    def withheld(bit, turn):
        return served(turn) & (pair == bit - 1)

    def answered(bit, turn):
        return served(turn) & (pair == 2 * bit - 1)

    def ask_copy(index):
        return pltpu.make_async_remote_copy(
            src_ref=q_hbm.at[:, columns(place(served_turn(index), side))],
            dst_ref=guest_q.at[index],
            send_sem=ask_send.at[index],
            recv_sem=ask_recv.at[index],
            device_id={"seq": host},
            device_id_type=pl.DeviceIdType.MESH,
        )

    def answer_copies(index):
        return [
            pltpu.make_async_remote_copy(
                src_ref=source.at[index],
                dst_ref=target.at[index],
                send_sem=answer_send.at[index, part],
                recv_sem=answer_recv.at[index, part],
                device_id={"seq": guest},
                device_id_type=pl.DeviceIdType.MESH,
            )
            for part, (source, target) in enumerate(((served_out, served_in), (stats_out, stats_in)))
        ]

    loads = [
        pltpu.make_async_copy(source, target, load_sem.at[index])
        for index, (source, target) in enumerate(
            ((k_hbm, k_ref), (v_hbm, v_ref), (q_hbm, q_ref), (len_hbm, len_ref), (scale_hbm, scale_ref))
        )
    ]
    for load in loads:
        load.start()
    barrier = pltpu.get_barrier_semaphore()
    greeted = partners + [above, below]
    for other in greeted:
        pl.semaphore_signal(
            barrier, inc=1, device_id={"seq": other}, device_id_type=pl.DeviceIdType.MESH
        )
    pl.semaphore_wait(barrier, len(greeted))

    def unless(condition, action):
        if condition is False:
            action()
        else:
            pl.when(jnp.logical_not(condition))(action)

    def send_far(turn):
        for bit in range(1, levels):
            def start(bit=bit):
                for part in range(2):
                    block_copy(bit, turn, part, side).start()

            unless(withheld(bit, turn) if serve else False, start)

    def send_near(turn, _):
        for part in range(2):
            block_copy(0, turn, part, 1 - side).start()
        return 0

    if serve:
        @pl.when(lax.rem(pair, 2) == 1)
        def _():
            for index in range(serve):
                ask_copy(index).start()

    lax.fori_loop(0, min(window, chunks), lambda turn, _: (send_far(turn), 0)[1], 0)
    lax.fori_loop(0, chunks, send_near, 0)

    row_ids = lax.broadcasted_iota(jnp.int32, (rows, rows), 0)
    column_ids = lax.broadcasted_iota(jnp.int32, (rows, rows), 1)
    live_rows = lax.broadcasted_iota(jnp.int32, (rows, width), 0)
    root = 1.0 / math.sqrt(width)

    for load in loads:
        load.wait()
    lengths = [len_ref[me]] + [len_ref[partner] for partner in partners]

    def head_columns(head):
        return pl.ds(pl.multiple_of(head * width, width), width)

    def key_value_sum(keys, values, length):
        mapped = jnp.where(live_rows < length, feature(keys.astype(jnp.float32)), 0.0)
        return sum(
            lax.dot_general(
                term, values, (((0,), (0,)), ((), ())), preferred_element_type=jnp.float32
            )
            for term in two_terms(mapped)
        )

    def piece(queries, keys, values, length, causal):
        scores = root * lax.dot_general(
            queries, keys, (((1,), (1,)), ((), ())), preferred_element_type=jnp.float32
        )
        allowed = column_ids < length
        if causal:
            allowed = allowed & (column_ids <= row_ids)
        peak = jnp.max(jnp.where(allowed, scores, -jnp.inf), axis=1, keepdims=True)
        weights = jnp.where(allowed, jnp.exp(scores - peak), 0.0).astype(jnp.bfloat16)
        total = jnp.sum(weights.astype(jnp.float32), axis=1, keepdims=True)
        numerator = jnp.dot(weights, values, preferred_element_type=jnp.float32)
        return numerator, peak, total

    def merge(pieces):
        top = functools.reduce(jnp.maximum, [peak for _, peak, _ in pieces])
        numerator, denominator = 0.0, 0.0
        for part, peak, total in pieces:
            factor = jnp.exp(peak - top)
            numerator = numerator + factor * part
            denominator = denominator + factor * total
        return numerator / denominator

    def attend(turn, finishing, asked):
        chunk = place(turn, side)
        cuts = [head_columns(chunk * per_chunk + offset) for offset in range(per_chunk)]
        pieces = [
            [
                piece(q_ref[:, cut], k_ref[:, cut], v_ref[:, cut], lengths[0], True),
                piece(q_ref[:, cut], far[0, 0, :, cut], far[0, 1, :, cut], lengths[1], False),
            ]
            for cut in cuts
        ]
        if asked:
            index = served_index(turn)
            for copy in answer_copies(index):
                copy.wait_recv()
            columns_of = jnp.tile(stats_in[index], (rows // 8, 1)).T
            for offset, found in enumerate(pieces):
                part = served_in[index, :, offset * width:(offset + 1) * width].astype(jnp.float32)
                at = 2 * offset
                found.append((part, columns_of[:, at:at + 1], columns_of[:, at + 1:at + 2]))
            remaining = [jnp.where(pair == 1, 2, 1)]
            extents = [jnp.where(pair == 1, lengths[3], lengths[2])]
        else:
            remaining = range(1, levels)
            extents = lengths[2:]
        for bit, extent in zip(remaining, extents):
            for part in range(2):
                block_copy(bit, turn, part, side).wait_recv()
            for cut, found in zip(cuts, pieces):
                found.append(piece(q_ref[:, cut], far[bit, 0, :, cut], far[bit, 1, :, cut], extent, False))
        for cut, found in zip(cuts, pieces):
            attention = merge(found)
            if finishing:
                out_ref[:, cut] = (attention + acc[:, cut]).astype(out_ref.dtype)
            else:
                acc[:, cut] = attention

    def answer(index):
        ask_copy(index).wait_recv()
        chunk = place(served_turn(index), side)
        lanes = jnp.zeros((rows, rows), jnp.float32)
        for offset in range(per_chunk):
            cut = head_columns(chunk * per_chunk + offset)
            local = slice(offset * width, (offset + 1) * width)
            numerator, peak, total = piece(
                guest_q[index, :, local], k_ref[:, cut], v_ref[:, cut], lengths[0], False
            )
            served_out[index, :, local] = numerator.astype(jnp.bfloat16)
            lanes = jnp.where(column_ids == 2 * offset, peak, lanes)
            lanes = jnp.where(column_ids == 2 * offset + 1, total, lanes)
        stats_out[index] = lanes.T[:8]
        for copy in answer_copies(index):
            copy.start()

    def add_linear(head, prefix, finishing):
        cut = head_columns(head)
        near = jnp.where(side > 0, near_sums[head], 0.0)
        prefix = jnp.where(pair > 0, prefix.astype(jnp.float32), 0.0) + near
        coarse, fine = two_terms(feature(q_ref[:, cut].astype(jnp.float32)))
        sums, rest = two_terms(prefix)
        linear = sum(
            jnp.dot(left, right, preferred_element_type=jnp.float32)
            for left, right in ((coarse, sums), (fine, sums), (coarse, rest))
        )
        gain = scale_ref[head] / (width * math.sqrt(rows * blocks))
        linear = gain * linear
        if finishing:
            out_ref[:, cut] = (acc[:, cut] + linear).astype(out_ref.dtype)
        else:
            acc[:, cut] = linear

    def one_turn(turn, _):
        @pl.when(turn < chunks)
        def _():
            chunk = place(turn, side)
            for part in range(2):
                block_copy(0, turn, part, side).wait_recv()
            for offset in range(per_chunk):
                head = chunk * per_chunk + offset
                cut = head_columns(head)
                near_sums[head] = key_value_sum(far[0, 0, :, cut], far[0, 1, :, cut], lengths[1])

            @pl.when(turn < half)
            def _():
                for offset in range(per_chunk):
                    cut = head_columns(chunk * per_chunk + offset)
                    own_sums[turn * per_chunk + offset] = key_value_sum(
                        k_ref[:, cut], v_ref[:, cut], lengths[0]
                    )

        link = turn - delay(pair)

        @pl.when((link >= 0) & (link < half))
        def _():
            first = place(link, side) * per_chunk

            @pl.when(pair > 0)
            def _():
                chain_copy(link).wait_recv()
                swap_copy(link).start()

            @pl.when(pair < pairs - 1)
            def _():
                for offset in range(per_chunk):
                    both = own_sums[link * per_chunk + offset] + near_sums[first + offset]
                    before = jnp.where(pair > 0, chain_in[link, offset].astype(jnp.float32), 0.0)
                    chain_out[link, offset] = (both + before).astype(jnp.bfloat16)
                chain_copy(link).start()

        @pl.when(turn + window < chunks)
        def _():
            send_far(turn + window)

        late = turn - linear_lag

        @pl.when((late >= 0) & (late < half))
        def _():
            @pl.when(pair > 0)
            def _():
                swap_copy(late).wait_recv()

            for offset in range(per_chunk):
                add_linear(place(late, side) * per_chunk + offset, chain_in[late, offset], True)
                add_linear(place(late, 1 - side) * per_chunk + offset, swap_in[late, offset], not linear_first)

        if serve:
            @pl.when((pair < pairs // 2) & (lax.rem(turn, 2) == 1) & (turn // 2 < serve))
            def _():
                answer(turn // 2)

        asking = served(turn) & (lax.rem(pair, 2) == 1)
        second = (turn >= half) & (turn < chunks)
        pl.when(turn < half)(lambda: attend(turn, False, False))
        if serve:
            pl.when(second & jnp.logical_not(asking))(lambda: attend(turn, linear_first, False))
            pl.when(second & asking)(lambda: attend(turn, linear_first, True))
        else:
            pl.when(second)(lambda: attend(turn, linear_first, False))

        return 0

    @pl.when(pair == 0)
    def _():
        def clear(turn, _):
            chain_in[turn] = jnp.zeros_like(chain_in[turn])
            swap_in[turn] = jnp.zeros_like(swap_in[turn])
            return 0

        lax.fori_loop(0, half, clear, 0)

    lax.fori_loop(0, turns, one_turn, 0)

    def finish(turn, _):
        for part in range(2):
            block_copy(0, turn, part, 1 - side).wait_send()
        for bit in range(1, levels):
            def wait(bit=bit):
                for part in range(2):
                    block_copy(bit, turn, part, side).wait_send()

            unless(withheld(bit, turn) if serve else False, wait)
        return 0

    lax.fori_loop(0, chunks, finish, 0)

    def finish_chain(turn, _):
        @pl.when(pair < pairs - 1)
        def _():
            chain_copy(turn).wait_send()

        @pl.when(pair > 0)
        def _():
            swap_copy(turn).wait_send()

        return 0

    lax.fori_loop(0, half, finish_chain, 0)

    def finish_served(index, _):
        @pl.when(lax.rem(pair, 2) == 1)
        def _():
            ask_copy(index).wait_send()

        @pl.when(pair < pairs // 2)
        def _():
            for copy in answer_copies(index):
                copy.wait_send()

        return 0

    lax.fori_loop(0, serve, finish_served, 0)


def delay(pair):
    return (LAG_TIMES * pair + 1) // LAG_OVER


def shards(blocks, query_rows, key_rows, value_rows, key_len, linear_scale):
    rows, total = query_rows.shape
    heads = linear_scale.shape[0]
    width = total // heads
    levels = blocks.bit_length() - 1
    chunks = heads // HEADS_PER_CHUNK
    half = chunks // 2
    serve = half // 2 if blocks == 8 else 0
    guests = max(serve, 1)
    span = HEADS_PER_CHUNK * width
    vmem = pl.BlockSpec(memory_space=pltpu.VMEM)
    hbm = pl.BlockSpec(memory_space=pltpu.HBM)
    piece = (half, HEADS_PER_CHUNK, width, width)
    dma = pltpu.SemaphoreType.DMA
    return pl.pallas_call(
        functools.partial(kernel, blocks, heads, width, HEADS_PER_CHUNK, WINDOW, delay, serve),
        out_shape=jax.ShapeDtypeStruct((rows, total), query_rows.dtype),
        in_specs=[hbm, hbm, hbm, hbm, hbm],
        out_specs=vmem,
        scratch_shapes=[
            pltpu.SMEM((blocks,), jnp.int32),
            pltpu.SMEM((heads,), jnp.float32),
            pltpu.VMEM((rows, total), jnp.bfloat16),
            pltpu.VMEM((rows, total), jnp.bfloat16),
            pltpu.VMEM((rows, total), jnp.bfloat16),
            dma((5,)),
            pltpu.VMEM((levels, 2, rows, total), jnp.bfloat16),
            pltpu.VMEM((rows, total), jnp.float32),
            pltpu.VMEM((heads // 2, width, width), jnp.float32),
            pltpu.VMEM((heads, width, width), jnp.float32),
            pltpu.VMEM(piece, jnp.bfloat16),
            pltpu.VMEM(piece, jnp.bfloat16),
            pltpu.VMEM(piece, jnp.bfloat16),
            dma((levels, chunks, 2)),
            dma((levels, chunks, 2)),
            dma((half,)),
            dma((half,)),
            dma((half,)),
            dma((half,)),
            pltpu.VMEM((guests, rows, span), jnp.bfloat16),
            pltpu.VMEM((guests, rows, span), jnp.bfloat16),
            pltpu.VMEM((guests, rows, span), jnp.bfloat16),
            pltpu.VMEM((guests, 8, rows), jnp.float32),
            pltpu.VMEM((guests, 8, rows), jnp.float32),
            dma((guests,)),
            dma((guests,)),
            dma((guests, 2)),
            dma((guests, 2)),
        ],
        compiler_params=pltpu.CompilerParams(
            collective_id=0, has_side_effects=True, vmem_limit_bytes=55000000
        ),
        name="butterfly",
    )(key_len, linear_scale, query_rows, key_rows, value_rows)


def solution(mesh):
    return jax.shard_map(
        functools.partial(shards, mesh.shape["seq"]),
        mesh=mesh,
        in_specs=(
            P(("groups", "seq"), "head"),
            P(("groups", "seq"), "head"),
            P(("groups", "seq"), "head"),
            P("groups"),
            P("head"),
        ),
        out_specs=P(("groups", "seq"), "head"),
        check_vma=False,
    )
```

```python
import functools
import math

import jax
import jax.numpy as jnp
from jax import lax
from jax.experimental import pallas as pl
from jax.experimental.pallas import tpu as pltpu
from jax.sharding import PartitionSpec as P

HEADS_PER_CHUNK = 2
WINDOW = 3
LAG_TIMES = 5
LAG_OVER = 3


def feature(inputs):
    return jnp.where(inputs > 0.0, inputs + 1.0, jnp.exp(jnp.minimum(inputs, 0.0)))


def two_terms(wide):
    coarse = wide.astype(jnp.bfloat16)
    return coarse, (wide - coarse.astype(jnp.float32)).astype(jnp.bfloat16)


def kernel(
    blocks, heads, width, per_chunk, window, delay, serve,
    len_hbm, scale_hbm, q_hbm, k_hbm, v_hbm, out_ref,
    len_ref, scale_ref, q_ref, k_ref, v_ref, load_sem, far, acc, own_sums, near_sums, chain_out, chain_in, swap_in,
    send_sem, recv_sem, chain_send, chain_recv, swap_send, swap_recv,
    guest_q, served_out, served_in, stats_out, stats_in, ask_send, ask_recv, answer_send, answer_recv,
):
    rows = q_ref.shape[0]
    levels = blocks.bit_length() - 1
    chunks = heads // per_chunk
    half = chunks // 2
    pairs = blocks // 2
    span = per_chunk * width
    linear_lag = max(half, delay(pairs - 1) + 1)
    linear_first = linear_lag == half
    turns = max(chunks, half + linear_lag)

    me = lax.axis_index("seq")
    side = lax.rem(me, 2)
    pair = me // 2
    partners = [me + (1 - 2 * lax.rem(me // (1 << bit), 2)) * (1 << bit) for bit in range(levels)]
    above = lax.rem(me + 2, blocks)
    below = lax.rem(me + blocks - 2, blocks)

    def place(turn, which):
        return lax.rem(turn + half * which, chunks)

    def columns(chunk):
        return pl.ds(pl.multiple_of(chunk * span, span), span)

    def block_copy(bit, turn, part, which):
        source = k_hbm if part == 0 else v_hbm
        cut = columns(place(turn, which))
        return pltpu.make_async_remote_copy(
            src_ref=source.at[:, cut],
            dst_ref=far.at[bit, part, :, cut],
            send_sem=send_sem.at[bit, turn, part],
            recv_sem=recv_sem.at[bit, turn, part],
            device_id={"seq": partners[bit] if isinstance(bit, int) else partners[1]},
            device_id_type=pl.DeviceIdType.MESH,
        )

    def chain_copy(turn):
        return pltpu.make_async_remote_copy(
            src_ref=chain_out.at[turn],
            dst_ref=chain_in.at[turn],
            send_sem=chain_send.at[turn],
            recv_sem=chain_recv.at[turn],
            device_id={"seq": above},
            device_id_type=pl.DeviceIdType.MESH,
        )

    def swap_copy(turn):
        return pltpu.make_async_remote_copy(
            src_ref=chain_in.at[turn],
            dst_ref=swap_in.at[turn],
            send_sem=swap_send.at[turn],
            recv_sem=swap_recv.at[turn],
            device_id={"seq": partners[0]},
            device_id_type=pl.DeviceIdType.MESH,
        )

    host = jnp.where(pair == 1, below, partners[-1])
    guest = jnp.where(pair == 0, above, partners[-1])

    def served(turn):
        return (turn >= half) & (lax.rem(turn, 2) == 1) if serve else False

    def served_turn(index):
        return half + 1 - half % 2 + 2 * index

    def served_index(turn):
        return (turn - half) // 2

    def withheld(bit, turn):
        return served(turn) & (pair == bit - 1)

    def answered(bit, turn):
        return served(turn) & (pair == 2 * bit - 1)

    def ask_copy(index):
        return pltpu.make_async_remote_copy(
            src_ref=q_hbm.at[:, columns(place(served_turn(index), side))],
            dst_ref=guest_q.at[index],
            send_sem=ask_send.at[index],
            recv_sem=ask_recv.at[index],
            device_id={"seq": host},
            device_id_type=pl.DeviceIdType.MESH,
        )

    def answer_copies(index):
        return [
            pltpu.make_async_remote_copy(
                src_ref=source.at[index],
                dst_ref=target.at[index],
                send_sem=answer_send.at[index, part],
                recv_sem=answer_recv.at[index, part],
                device_id={"seq": guest},
                device_id_type=pl.DeviceIdType.MESH,
            )
            for part, (source, target) in enumerate(((served_out, served_in), (stats_out, stats_in)))
        ]

    loads = [
        pltpu.make_async_copy(source, target, load_sem.at[index])
        for index, (source, target) in enumerate(
            ((k_hbm, k_ref), (v_hbm, v_ref), (q_hbm, q_ref), (len_hbm, len_ref), (scale_hbm, scale_ref))
        )
    ]
    for load in loads:
        load.start()
    barrier = pltpu.get_barrier_semaphore()
    greeted = partners + [above, below]
    for other in greeted:
        pl.semaphore_signal(
            barrier, inc=1, device_id={"seq": other}, device_id_type=pl.DeviceIdType.MESH
        )
    pl.semaphore_wait(barrier, len(greeted))

    def unless(condition, action):
        if condition is False:
            action()
        else:
            pl.when(jnp.logical_not(condition))(action)

    def send_far(turn):
        for bit in range(1, levels):
            def start(bit=bit):
                for part in range(2):
                    block_copy(bit, turn, part, side).start()

            unless(withheld(bit, turn) if serve else False, start)

    def send_near(turn, _):
        for part in range(2):
            block_copy(0, turn, part, 1 - side).start()
        return 0

    if serve:
        @pl.when(lax.rem(pair, 2) == 1)
        def _():
            for index in range(serve):
                ask_copy(index).start()

    lax.fori_loop(0, min(window, chunks), lambda turn, _: (send_far(turn), 0)[1], 0)
    lax.fori_loop(0, chunks, send_near, 0)

    row_ids = lax.broadcasted_iota(jnp.int32, (rows, rows), 0)
    column_ids = lax.broadcasted_iota(jnp.int32, (rows, rows), 1)
    live_rows = lax.broadcasted_iota(jnp.int32, (rows, width), 0)
    root = 1.0 / math.sqrt(width)

    for load in loads:
        load.wait()
    lengths = [len_ref[me]] + [len_ref[partner] for partner in partners]

    def head_columns(head):
        return pl.ds(pl.multiple_of(head * width, width), width)

    def key_value_sum(keys, values, length):
        mapped = jnp.where(live_rows < length, feature(keys.astype(jnp.float32)), 0.0)
        return sum(
            lax.dot_general(
                term, values, (((0,), (0,)), ((), ())), preferred_element_type=jnp.float32
            )
            for term in two_terms(mapped)
        )

    def piece(queries, keys, values, length, causal):
        scores = root * lax.dot_general(
            queries, keys, (((1,), (1,)), ((), ())), preferred_element_type=jnp.float32
        )
        allowed = column_ids < length
        if causal:
            allowed = allowed & (column_ids <= row_ids)
        peak = jnp.max(jnp.where(allowed, scores, -jnp.inf), axis=1, keepdims=True)
        weights = jnp.where(allowed, jnp.exp(scores - peak), 0.0).astype(jnp.bfloat16)
        total = jnp.sum(weights.astype(jnp.float32), axis=1, keepdims=True)
        numerator = jnp.dot(weights, values, preferred_element_type=jnp.float32)
        return numerator, peak, total

    def merge(pieces):
        top = functools.reduce(jnp.maximum, [peak for _, peak, _ in pieces])
        numerator, denominator = 0.0, 0.0
        for part, peak, total in pieces:
            factor = jnp.exp(peak - top)
            numerator = numerator + factor * part
            denominator = denominator + factor * total
        return numerator / denominator

    def attend(turn, finishing, asked):
        chunk = place(turn, side)
        cuts = [head_columns(chunk * per_chunk + offset) for offset in range(per_chunk)]
        pieces = [
            [
                piece(q_ref[:, cut], k_ref[:, cut], v_ref[:, cut], lengths[0], True),
                piece(q_ref[:, cut], far[0, 0, :, cut], far[0, 1, :, cut], lengths[1], False),
            ]
            for cut in cuts
        ]
        if asked:
            index = served_index(turn)
            for copy in answer_copies(index):
                copy.wait_recv()
            columns_of = jnp.tile(stats_in[index], (rows // 8, 1)).T
            for offset, found in enumerate(pieces):
                part = served_in[index, :, offset * width:(offset + 1) * width].astype(jnp.float32)
                at = 2 * offset
                found.append((part, columns_of[:, at:at + 1], columns_of[:, at + 1:at + 2]))
            remaining = [jnp.where(pair == 1, 2, 1)]
            extents = [jnp.where(pair == 1, lengths[3], lengths[2])]
        else:
            remaining = range(1, levels)
            extents = lengths[2:]
        for bit, extent in zip(remaining, extents):
            for part in range(2):
                block_copy(bit, turn, part, side).wait_recv()
            for cut, found in zip(cuts, pieces):
                found.append(piece(q_ref[:, cut], far[bit, 0, :, cut], far[bit, 1, :, cut], extent, False))
        for cut, found in zip(cuts, pieces):
            attention = merge(found)
            if finishing:
                out_ref[:, cut] = (attention + acc[:, cut]).astype(out_ref.dtype)
            else:
                acc[:, cut] = attention

    def answer(index):
        ask_copy(index).wait_recv()
        chunk = place(served_turn(index), side)
        lanes = jnp.zeros((rows, rows), jnp.float32)
        for offset in range(per_chunk):
            cut = head_columns(chunk * per_chunk + offset)
            local = slice(offset * width, (offset + 1) * width)
            numerator, peak, total = piece(
                guest_q[index, :, local], k_ref[:, cut], v_ref[:, cut], lengths[0], False
            )
            served_out[index, :, local] = numerator.astype(jnp.bfloat16)
            lanes = jnp.where(column_ids == 2 * offset, peak, lanes)
            lanes = jnp.where(column_ids == 2 * offset + 1, total, lanes)
        stats_out[index] = lanes.T[:8]
        for copy in answer_copies(index):
            copy.start()

    def add_linear(head, prefix, finishing):
        cut = head_columns(head)
        near = jnp.where(side > 0, near_sums[head], 0.0)
        prefix = jnp.where(pair > 0, prefix.astype(jnp.float32), 0.0) + near
        coarse, fine = two_terms(feature(q_ref[:, cut].astype(jnp.float32)))
        sums, rest = two_terms(prefix)
        linear = sum(
            jnp.dot(left, right, preferred_element_type=jnp.float32)
            for left, right in ((coarse, sums), (fine, sums), (coarse, rest))
        )
        gain = scale_ref[head] / (width * math.sqrt(rows * blocks))
        linear = gain * linear
        if finishing:
            out_ref[:, cut] = (acc[:, cut] + linear).astype(out_ref.dtype)
        else:
            acc[:, cut] = linear

    def one_turn(turn, _):
        @pl.when(turn < chunks)
        def _():
            chunk = place(turn, side)
            for part in range(2):
                block_copy(0, turn, part, side).wait_recv()
            for offset in range(per_chunk):
                head = chunk * per_chunk + offset
                cut = head_columns(head)
                near_sums[head] = key_value_sum(far[0, 0, :, cut], far[0, 1, :, cut], lengths[1])

            @pl.when(turn < half)
            def _():
                for offset in range(per_chunk):
                    cut = head_columns(chunk * per_chunk + offset)
                    own_sums[turn * per_chunk + offset] = key_value_sum(
                        k_ref[:, cut], v_ref[:, cut], lengths[0]
                    )

        link = turn - delay(pair)

        @pl.when((link >= 0) & (link < half))
        def _():
            first = place(link, side) * per_chunk

            @pl.when(pair > 0)
            def _():
                chain_copy(link).wait_recv()
                swap_copy(link).start()

            @pl.when(pair < pairs - 1)
            def _():
                for offset in range(per_chunk):
                    both = own_sums[link * per_chunk + offset] + near_sums[first + offset]
                    before = jnp.where(pair > 0, chain_in[link, offset].astype(jnp.float32), 0.0)
                    chain_out[link, offset] = (both + before).astype(jnp.bfloat16)
                chain_copy(link).start()

        @pl.when(turn + window < chunks)
        def _():
            send_far(turn + window)

        late = turn - linear_lag

        @pl.when((late >= 0) & (late < half))
        def _():
            @pl.when(pair > 0)
            def _():
                swap_copy(late).wait_recv()

            for offset in range(per_chunk):
                add_linear(place(late, side) * per_chunk + offset, chain_in[late, offset], True)
                add_linear(place(late, 1 - side) * per_chunk + offset, swap_in[late, offset], not linear_first)

        if serve:
            @pl.when((pair < pairs // 2) & (lax.rem(turn, 2) == 1) & (turn // 2 < serve))
            def _():
                answer(turn // 2)

        asking = served(turn) & (lax.rem(pair, 2) == 1)
        second = (turn >= half) & (turn < chunks)
        pl.when(turn < half)(lambda: attend(turn, False, False))
        if serve:
            pl.when(second & jnp.logical_not(asking))(lambda: attend(turn, linear_first, False))
            pl.when(second & asking)(lambda: attend(turn, linear_first, True))
        else:
            pl.when(second)(lambda: attend(turn, linear_first, False))

        return 0

    @pl.when(pair == 0)
    def _():
        def clear(turn, _):
            chain_in[turn] = jnp.zeros_like(chain_in[turn])
            swap_in[turn] = jnp.zeros_like(swap_in[turn])
            return 0

        lax.fori_loop(0, half, clear, 0)

    lax.fori_loop(0, turns, one_turn, 0)

    def finish(turn, _):
        for part in range(2):
            block_copy(0, turn, part, 1 - side).wait_send()
        for bit in range(1, levels):
            def wait(bit=bit):
                for part in range(2):
                    block_copy(bit, turn, part, side).wait_send()

            unless(withheld(bit, turn) if serve else False, wait)
        return 0

    lax.fori_loop(0, chunks, finish, 0)

    def finish_chain(turn, _):
        @pl.when(pair < pairs - 1)
        def _():
            chain_copy(turn).wait_send()

        @pl.when(pair > 0)
        def _():
            swap_copy(turn).wait_send()

        return 0

    lax.fori_loop(0, half, finish_chain, 0)

    def finish_served(index, _):
        @pl.when(lax.rem(pair, 2) == 1)
        def _():
            ask_copy(index).wait_send()

        @pl.when(pair < pairs // 2)
        def _():
            for copy in answer_copies(index):
                copy.wait_send()

        return 0

    lax.fori_loop(0, serve, finish_served, 0)


def delay(pair):
    return (LAG_TIMES * pair + 1) // LAG_OVER


def shards(blocks, query_rows, key_rows, value_rows, key_len, linear_scale):
    rows, total = query_rows.shape
    heads = linear_scale.shape[0]
    width = total // heads
    levels = blocks.bit_length() - 1
    chunks = heads // HEADS_PER_CHUNK
    half = chunks // 2
    serve = half // 2 if blocks == 8 else 0
    guests = max(serve, 1)
    span = HEADS_PER_CHUNK * width
    vmem = pl.BlockSpec(memory_space=pltpu.VMEM)
    hbm = pl.BlockSpec(memory_space=pltpu.HBM)
    piece = (half, HEADS_PER_CHUNK, width, width)
    dma = pltpu.SemaphoreType.DMA
    return pl.pallas_call(
        functools.partial(kernel, blocks, heads, width, HEADS_PER_CHUNK, WINDOW, delay, serve),
        out_shape=jax.ShapeDtypeStruct((rows, total), query_rows.dtype),
        in_specs=[hbm, hbm, hbm, hbm, hbm],
        out_specs=vmem,
        scratch_shapes=[
            pltpu.SMEM((blocks,), jnp.int32),
            pltpu.SMEM((heads,), jnp.float32),
            pltpu.VMEM((rows, total), jnp.bfloat16),
            pltpu.VMEM((rows, total), jnp.bfloat16),
            pltpu.VMEM((rows, total), jnp.bfloat16),
            dma((5,)),
            pltpu.VMEM((levels, 2, rows, total), jnp.bfloat16),
            pltpu.VMEM((rows, total), jnp.float32),
            pltpu.VMEM((heads // 2, width, width), jnp.float32),
            pltpu.VMEM((heads, width, width), jnp.float32),
            pltpu.VMEM(piece, jnp.bfloat16),
            pltpu.VMEM(piece, jnp.bfloat16),
            pltpu.VMEM(piece, jnp.bfloat16),
            dma((levels, chunks, 2)),
            dma((levels, chunks, 2)),
            dma((half,)),
            dma((half,)),
            dma((half,)),
            dma((half,)),
            pltpu.VMEM((guests, rows, span), jnp.bfloat16),
            pltpu.VMEM((guests, rows, span), jnp.bfloat16),
            pltpu.VMEM((guests, rows, span), jnp.bfloat16),
            pltpu.VMEM((guests, 8, rows), jnp.float32),
            pltpu.VMEM((guests, 8, rows), jnp.float32),
            dma((guests,)),
            dma((guests,)),
            dma((guests, 2)),
            dma((guests, 2)),
        ],
        compiler_params=pltpu.CompilerParams(
            collective_id=0, has_side_effects=True, vmem_limit_bytes=55000000
        ),
        name="butterfly",
    )(
        pltpu.with_memory_space_constraint(key_len, pltpu.HBM),
        pltpu.with_memory_space_constraint(linear_scale, pltpu.HBM),
        query_rows, key_rows, value_rows,
    )


def solution(mesh):
    return jax.shard_map(
        functools.partial(shards, mesh.shape["seq"]),
        mesh=mesh,
        in_specs=(
            P(("groups", "seq"), "head"),
            P(("groups", "seq"), "head"),
            P(("groups", "seq"), "head"),
            P("groups"),
            P("head"),
        ),
        out_specs=P(("groups", "seq"), "head"),
        check_vma=False,
    )
```

```python
import functools
import math

import jax
import jax.numpy as jnp
from jax import lax
from jax.experimental import pallas as pl
from jax.experimental.pallas import tpu as pltpu
from jax.sharding import PartitionSpec as P

HEADS_PER_CHUNK = 2
WINDOW = 2
STEPS = 2
CALM = 3
SERVED = 5
LAG_TIMES = 6
LAG_OVER = 3


def feature(inputs):
    return jnp.where(inputs > 0.0, inputs + 1.0, jnp.exp(jnp.minimum(inputs, 0.0)))


def two_terms(wide):
    coarse = wide.astype(jnp.bfloat16)
    return coarse, (wide - coarse.astype(jnp.float32)).astype(jnp.bfloat16)


def kernel(
    blocks, heads, width, per_chunk, window, calm, delay, serve,
    len_hbm, scale_hbm, q_hbm, k_hbm, v_hbm, out_ref,
    len_ref, scale_ref, q_ref, k_ref, v_ref, load_sem, far, acc, own_sums, near_sums, chain_out, chain_in, swap_in,
    send_sem, recv_sem, chain_send, chain_recv, swap_send, swap_recv,
    guest_q, served_out, served_in, stats_out, stats_in, ask_send, ask_recv, answer_send, answer_recv,
):
    rows = q_ref.shape[0]
    levels = blocks.bit_length() - 1
    chunks = heads // per_chunk
    half = chunks // 2
    pairs = blocks // 2
    span = per_chunk * width
    rounds = pl.cdiv(half, STEPS)
    linear_lag = max(chunks - rounds, delay(pairs - 1) + 1)
    joined = linear_lag + rounds == chunks
    turns = linear_lag + rounds

    me = lax.axis_index("seq")
    side = lax.rem(me, 2)
    pair = me // 2
    partners = [me + (1 - 2 * lax.rem(me // (1 << bit), 2)) * (1 << bit) for bit in range(levels)]
    above = lax.rem(me + 2, blocks)
    below = lax.rem(me + blocks - 2, blocks)

    def place(turn, which):
        return lax.rem(turn + half * which, chunks)

    def columns(chunk):
        return pl.ds(pl.multiple_of(chunk * span, span), span)

    def head_columns(head):
        return pl.ds(pl.multiple_of(head * width, width), width)

    def block_copy(bit, turn, part, which, heads_sent=per_chunk):
        source = k_hbm if part == 0 else v_hbm
        cut = pl.ds(pl.multiple_of(place(turn, which) * span, span), heads_sent * width)
        return pltpu.make_async_remote_copy(
            src_ref=source.at[:, cut],
            dst_ref=far.at[bit, part, :, cut],
            send_sem=send_sem.at[bit, turn, part],
            recv_sem=recv_sem.at[bit, turn, part],
            device_id={"seq": partners[bit] if isinstance(bit, int) else partners[1]},
            device_id_type=pl.DeviceIdType.MESH,
        )

    def chain_copy(turn):
        return pltpu.make_async_remote_copy(
            src_ref=chain_out.at[turn],
            dst_ref=chain_in.at[turn],
            send_sem=chain_send.at[turn],
            recv_sem=chain_recv.at[turn],
            device_id={"seq": above},
            device_id_type=pl.DeviceIdType.MESH,
        )

    def swap_copy(turn):
        return pltpu.make_async_remote_copy(
            src_ref=chain_in.at[turn],
            dst_ref=swap_in.at[turn],
            send_sem=swap_send.at[turn],
            recv_sem=swap_recv.at[turn],
            device_id={"seq": partners[0]},
            device_id_type=pl.DeviceIdType.MESH,
        )

    host = jnp.where(pair == 1, below, partners[-1])
    guest = jnp.where(pair == 0, above, partners[-1])

    def served(turn):
        return (turn >= chunks - serve) & (turn < chunks) if serve else False

    def served_turn(index):
        return chunks - serve + index

    def served_index(turn):
        return turn - (chunks - serve)

    def withheld(bit, turn):
        return served(turn) & (pair == bit - 1)

    def ask_copy(index):
        return pltpu.make_async_remote_copy(
            src_ref=q_hbm.at[:, head_columns((place(served_turn(index), side) + 1) * per_chunk - 1)],
            dst_ref=guest_q.at[index],
            send_sem=ask_send.at[index],
            recv_sem=ask_recv.at[index],
            device_id={"seq": host},
            device_id_type=pl.DeviceIdType.MESH,
        )

    def answer_copies(index):
        return [
            pltpu.make_async_remote_copy(
                src_ref=source.at[index],
                dst_ref=target.at[index],
                send_sem=answer_send.at[index, part],
                recv_sem=answer_recv.at[index, part],
                device_id={"seq": guest},
                device_id_type=pl.DeviceIdType.MESH,
            )
            for part, (source, target) in enumerate(((served_out, served_in), (stats_out, stats_in)))
        ]

    loads = [
        pltpu.make_async_copy(source, target, load_sem.at[index])
        for index, (source, target) in enumerate(
            ((k_hbm, k_ref), (v_hbm, v_ref), (q_hbm, q_ref), (len_hbm, len_ref), (scale_hbm, scale_ref))
        )
    ]
    for load in loads:
        load.start()
    barrier = pltpu.get_barrier_semaphore()
    greeted = partners + [above, below]
    for other in greeted:
        pl.semaphore_signal(
            barrier, inc=1, device_id={"seq": other}, device_id_type=pl.DeviceIdType.MESH
        )
    pl.semaphore_wait(barrier, len(greeted))

    def for_each_far(turn, action):
        for bit in range(1, levels):
            def whole(bit=bit):
                for part in range(2):
                    action(block_copy(bit, turn, part, side))

            def less(bit=bit):
                for part in range(2):
                    action(block_copy(bit, turn, part, side, per_chunk - 1))

            if serve:
                pl.when(jnp.logical_not(withheld(bit, turn)))(whole)
                pl.when(withheld(bit, turn))(less)
            else:
                whole()

    def send_far(turn):
        for_each_far(turn, lambda copy: copy.start())

    def send_near(turn, _):
        for part in range(2):
            block_copy(0, turn, part, 1 - side).start()
        return 0

    def sent_by(turn):
        more = jnp.maximum(turn - delay(pair) - calm, 0)
        return jnp.minimum(window + turn + 1 + more, chunks)

    if serve:
        @pl.when(lax.rem(pair, 2) == 1)
        def _():
            for index in range(serve):
                ask_copy(index).start()

    lax.fori_loop(0, sent_by(-1), lambda turn, _: (send_far(turn), 0)[1], 0)
    lax.fori_loop(0, chunks, send_near, 0)

    row_ids = lax.broadcasted_iota(jnp.int32, (rows, rows), 0)
    column_ids = lax.broadcasted_iota(jnp.int32, (rows, rows), 1)
    live_rows = lax.broadcasted_iota(jnp.int32, (rows, width), 0)
    root = 1.0 / math.sqrt(width)

    for load in loads:
        load.wait()
    lengths = [len_ref[me]] + [len_ref[partner] for partner in partners]

    def key_value_sum(keys, values, length):
        mapped = jnp.where(live_rows < length, feature(keys.astype(jnp.float32)), 0.0)
        return sum(
            lax.dot_general(
                term, values, (((0,), (0,)), ((), ())), preferred_element_type=jnp.float32
            )
            for term in two_terms(mapped)
        )

    def piece(queries, keys, values, length, causal):
        scores = root * lax.dot_general(
            queries, keys, (((1,), (1,)), ((), ())), preferred_element_type=jnp.float32
        )
        allowed = column_ids < length
        if causal:
            allowed = allowed & (column_ids <= row_ids)
        peak = jnp.max(jnp.where(allowed, scores, -jnp.inf), axis=1, keepdims=True)
        weights = jnp.where(allowed, jnp.exp(scores - peak), 0.0).astype(jnp.bfloat16)
        total = jnp.sum(weights.astype(jnp.float32), axis=1, keepdims=True)
        numerator = jnp.dot(weights, values, preferred_element_type=jnp.float32)
        return numerator, peak, total

    def merge(pieces):
        top = functools.reduce(jnp.maximum, [peak for _, peak, _ in pieces])
        numerator, denominator = 0.0, 0.0
        for part, peak, total in pieces:
            factor = jnp.exp(peak - top)
            numerator = numerator + factor * part
            denominator = denominator + factor * total
        return numerator / denominator

    def attend(turn, finishing, asked):
        chunk = place(turn, side)
        cuts = [head_columns(chunk * per_chunk + offset) for offset in range(per_chunk)]
        pieces = [
            [
                piece(q_ref[:, cut], k_ref[:, cut], v_ref[:, cut], lengths[0], True),
                piece(q_ref[:, cut], far[0, 0, :, cut], far[0, 1, :, cut], lengths[1], False),
            ]
            for cut in cuts
        ]
        if asked:
            full, cut_short = jnp.where(pair == 1, 2, 1), jnp.where(pair == 1, 1, 2)
            sources = [
                (full, jnp.where(pair == 1, lengths[3], lengths[2]), per_chunk),
                (cut_short, jnp.where(pair == 1, lengths[2], lengths[3]), per_chunk - 1),
            ]
            index = served_index(turn)
            for copy in answer_copies(index):
                copy.wait_recv()
            columns_of = jnp.tile(stats_in[index], (rows // 8, 1)).T
            pieces[-1].append((served_in[index].astype(jnp.float32), columns_of[:, :1], columns_of[:, 1:2]))
        else:
            sources = [(bit, lengths[1 + bit], per_chunk) for bit in range(1, levels)]
        for bit, extent, count in sources:
            for part in range(2):
                block_copy(bit, turn, part, side, count).wait_recv()
            for cut, found in list(zip(cuts, pieces))[:count]:
                found.append(piece(q_ref[:, cut], far[bit, 0, :, cut], far[bit, 1, :, cut], extent, False))
        for cut, found in zip(cuts, pieces):
            attention = merge(found)
            if finishing:
                out_ref[:, cut] = (attention + acc[:, cut]).astype(out_ref.dtype)
            else:
                acc[:, cut] = attention

    def answer(index):
        ask_copy(index).wait_recv()
        cut = head_columns((place(served_turn(index), side) + 1) * per_chunk - 1)
        numerator, peak, total = piece(guest_q[index], k_ref[:, cut], v_ref[:, cut], lengths[0], False)
        served_out[index] = numerator.astype(jnp.bfloat16)
        lanes = jnp.where(column_ids == 0, peak, total)
        stats_out[index] = lanes.T[:8]
        for copy in answer_copies(index):
            copy.start()

    def add_linear(head, prefix, finishing):
        cut = head_columns(head)
        near = jnp.where(side > 0, near_sums[head], 0.0)
        prefix = jnp.where(pair > 0, prefix.astype(jnp.float32), 0.0) + near
        coarse, fine = two_terms(feature(q_ref[:, cut].astype(jnp.float32)))
        sums, rest = two_terms(prefix)
        linear = sum(
            jnp.dot(left, right, preferred_element_type=jnp.float32)
            for left, right in ((coarse, sums), (fine, sums), (coarse, rest))
        )
        gain = scale_ref[head] / (width * math.sqrt(rows * blocks))
        linear = gain * linear
        if finishing:
            out_ref[:, cut] = (acc[:, cut] + linear).astype(out_ref.dtype)
        else:
            acc[:, cut] = linear

    def prepare(step):
        for part in range(2):
            block_copy(0, step, part, side).wait_recv()
        chunk = place(step, side)

        @pl.when((step < half) | (side > 0))
        def _():
            for offset in range(per_chunk):
                head = chunk * per_chunk + offset
                cut = head_columns(head)
                near_sums[head] = key_value_sum(far[0, 0, :, cut], far[0, 1, :, cut], lengths[1])

        @pl.when((step < half) & (pair < pairs - 1))
        def _():
            for offset in range(per_chunk):
                cut = head_columns(chunk * per_chunk + offset)
                own_sums[step * per_chunk + offset] = key_value_sum(k_ref[:, cut], v_ref[:, cut], lengths[0])

    def pass_on(link):
        first = place(link, side) * per_chunk

        @pl.when(pair > 0)
        def _():
            chain_copy(link).wait_recv()

        @pl.when(pair < pairs - 1)
        def _():
            for offset in range(per_chunk):
                both = own_sums[link * per_chunk + offset] + near_sums[first + offset]
                before = jnp.where(pair > 0, chain_in[link, offset].astype(jnp.float32), 0.0)
                chain_out[link, offset] = (both + before).astype(jnp.bfloat16)
            chain_copy(link).start()

        @pl.when(pair > 0)
        def _():
            swap_copy(link).start()

    def finish_linear(late):
        @pl.when(pair > 0)
        def _():
            swap_copy(late).wait_recv()

        for offset in range(per_chunk):
            add_linear(place(late, side) * per_chunk + offset, chain_in[late, offset], True)

        def other(finishing):
            for offset in range(per_chunk):
                add_linear(place(late, 1 - side) * per_chunk + offset, swap_in[late, offset], finishing)

        if joined:
            pl.when(late < half - 1)(lambda: other(True))
            pl.when(late == half - 1)(lambda: other(False))
        else:
            other(True)

    def steps(first, limit, action):
        for offset in range(STEPS):
            step = first * STEPS + offset
            pl.when((step >= 0) & (step < limit))(functools.partial(action, step))

    def one_turn(turn, _):
        steps(turn, chunks, prepare)
        steps(turn - delay(pair), half, pass_on)
        lax.fori_loop(sent_by(turn - 1), sent_by(turn), lambda chunk, _: (send_far(chunk), 0)[1], 0)
        steps(turn - linear_lag, half, finish_linear)

        if serve:
            @pl.when((pair < pairs // 2) & (turn > 0) & (turn <= serve))
            def _():
                answer(turn - 1)

        asking = served(turn) & (lax.rem(pair, 2) == 1)
        inside = turn < (chunks - 1 if joined else chunks)
        if serve:
            pl.when(inside & jnp.logical_not(asking))(lambda: attend(turn, False, False))
            pl.when(inside & asking)(lambda: attend(turn, False, True))
        else:
            pl.when(inside)(lambda: attend(turn, False, False))
        if joined:
            last = turn == chunks - 1
            if serve:
                pl.when(last & jnp.logical_not(asking))(lambda: attend(turn, True, False))
                pl.when(last & asking)(lambda: attend(turn, True, True))
            else:
                pl.when(last)(lambda: attend(turn, True, False))

        return 0

    @pl.when(pair == 0)
    def _():
        def clear(turn, _):
            chain_in[turn] = jnp.zeros_like(chain_in[turn])
            swap_in[turn] = jnp.zeros_like(swap_in[turn])
            return 0

        lax.fori_loop(0, half, clear, 0)

    lax.fori_loop(0, turns, one_turn, 0)

    def finish(turn, _):
        for part in range(2):
            block_copy(0, turn, part, 1 - side).wait_send()
        for_each_far(turn, lambda copy: copy.wait_send())
        return 0

    lax.fori_loop(0, chunks, finish, 0)

    def finish_chain(turn, _):
        @pl.when(pair < pairs - 1)
        def _():
            chain_copy(turn).wait_send()

        @pl.when(pair > 0)
        def _():
            swap_copy(turn).wait_send()

        return 0

    lax.fori_loop(0, half, finish_chain, 0)

    def finish_served(index, _):
        @pl.when(lax.rem(pair, 2) == 1)
        def _():
            ask_copy(index).wait_send()

        @pl.when(pair < pairs // 2)
        def _():
            for copy in answer_copies(index):
                copy.wait_send()

        return 0

    lax.fori_loop(0, serve, finish_served, 0)


def delay(pair):
    return (LAG_TIMES * pair + 1) // LAG_OVER


def shards(blocks, query_rows, key_rows, value_rows, key_len, linear_scale):
    rows, total = query_rows.shape
    heads = linear_scale.shape[0]
    width = total // heads
    levels = blocks.bit_length() - 1
    chunks = heads // HEADS_PER_CHUNK
    half = chunks // 2
    serve = SERVED if blocks == 8 else 0
    guests = max(serve, 1)
    vmem = pl.BlockSpec(memory_space=pltpu.VMEM)
    hbm = pl.BlockSpec(memory_space=pltpu.HBM)
    piece = (half, HEADS_PER_CHUNK, width, width)
    dma = pltpu.SemaphoreType.DMA
    return pl.pallas_call(
        functools.partial(kernel, blocks, heads, width, HEADS_PER_CHUNK, WINDOW, CALM, delay, serve),
        out_shape=jax.ShapeDtypeStruct((rows, total), query_rows.dtype),
        in_specs=[hbm, hbm, hbm, hbm, hbm],
        out_specs=vmem,
        scratch_shapes=[
            pltpu.SMEM((blocks,), jnp.int32),
            pltpu.SMEM((heads,), jnp.float32),
            pltpu.VMEM((rows, total), jnp.bfloat16),
            pltpu.VMEM((rows, total), jnp.bfloat16),
            pltpu.VMEM((rows, total), jnp.bfloat16),
            dma((5,)),
            pltpu.VMEM((levels, 2, rows, total), jnp.bfloat16),
            pltpu.VMEM((rows, total), jnp.float32),
            pltpu.VMEM((heads // 2, width, width), jnp.float32),
            pltpu.VMEM((heads, width, width), jnp.float32),
            pltpu.VMEM(piece, jnp.bfloat16),
            pltpu.VMEM(piece, jnp.bfloat16),
            pltpu.VMEM(piece, jnp.bfloat16),
            dma((levels, chunks, 2)),
            dma((levels, chunks, 2)),
            dma((half,)),
            dma((half,)),
            dma((half,)),
            dma((half,)),
            pltpu.VMEM((guests, rows, width), jnp.bfloat16),
            pltpu.VMEM((guests, rows, width), jnp.bfloat16),
            pltpu.VMEM((guests, rows, width), jnp.bfloat16),
            pltpu.VMEM((guests, 8, rows), jnp.float32),
            pltpu.VMEM((guests, 8, rows), jnp.float32),
            dma((guests,)),
            dma((guests,)),
            dma((guests, 2)),
            dma((guests, 2)),
        ],
        compiler_params=pltpu.CompilerParams(
            collective_id=0, has_side_effects=True, vmem_limit_bytes=55000000
        ),
        name="butterfly",
    )(
        pltpu.with_memory_space_constraint(key_len, pltpu.HBM),
        pltpu.with_memory_space_constraint(linear_scale, pltpu.HBM),
        query_rows, key_rows, value_rows,
    )


def solution(mesh):
    return jax.shard_map(
        functools.partial(shards, mesh.shape["seq"]),
        mesh=mesh,
        in_specs=(
            P(("groups", "seq"), "head"),
            P(("groups", "seq"), "head"),
            P(("groups", "seq"), "head"),
            P("groups"),
            P("head"),
        ),
        out_specs=P(("groups", "seq"), "head"),
        check_vma=False,
    )
```

```python
import functools
import math

import jax
import jax.numpy as jnp
from jax import lax
from jax.experimental import pallas as pl
from jax.experimental.pallas import tpu as pltpu
from jax.sharding import PartitionSpec as P

HEADS_PER_CHUNK = 2
WINDOW = 2
STEPS = 2
CALM = 3
SERVED = 5
LAG_TIMES = 6
LAG_OVER = 3


def feature(inputs):
    return jnp.where(inputs > 0.0, inputs + 1.0, jnp.exp(jnp.minimum(inputs, 0.0)))


def two_terms(wide):
    coarse = wide.astype(jnp.bfloat16)
    return coarse, (wide - coarse.astype(jnp.float32)).astype(jnp.bfloat16)


def kernel(
    blocks, heads, width, per_chunk, window, calm, delay, serve,
    len_hbm, scale_hbm, q_hbm, k_hbm, v_hbm, out_ref,
    len_ref, scale_ref, q_ref, k_ref, v_ref, load_sem, far, acc, own_sums, near_sums, chain_out, chain_in, swap_in,
    send_sem, recv_sem, chain_send, chain_recv, swap_send, swap_recv,
    guest_q, served_out, served_in, stats_out, stats_in, ask_send, ask_recv, answer_send, answer_recv,
):
    rows = q_ref.shape[0]
    levels = blocks.bit_length() - 1
    chunks = heads // per_chunk
    half = chunks // 2
    pairs = blocks // 2
    span = per_chunk * width
    rounds = pl.cdiv(half, STEPS)
    linear_lag = max(chunks - rounds, delay(pairs - 1) + 1)
    joined = linear_lag + rounds == chunks
    turns = linear_lag + rounds

    me = lax.axis_index("seq")
    side = lax.rem(me, 2)
    pair = me // 2
    partners = [me + (1 - 2 * lax.rem(me // (1 << bit), 2)) * (1 << bit) for bit in range(levels)]
    above = lax.rem(me + 2, blocks)
    below = lax.rem(me + blocks - 2, blocks)

    def place(turn, which):
        return lax.rem(turn + half * which, chunks)

    def columns(chunk):
        return pl.ds(pl.multiple_of(chunk * span, span), span)

    def head_columns(head):
        return pl.ds(pl.multiple_of(head * width, width), width)

    def block_copy(bit, turn, part, which, heads_sent=per_chunk):
        source = k_hbm if part == 0 else v_hbm
        cut = pl.ds(pl.multiple_of(place(turn, which) * span, span), heads_sent * width)
        return pltpu.make_async_remote_copy(
            src_ref=source.at[:, cut],
            dst_ref=far.at[bit, part, :, cut],
            send_sem=send_sem.at[bit, turn, part],
            recv_sem=recv_sem.at[bit, turn, part],
            device_id={"seq": partners[bit] if isinstance(bit, int) else partners[1]},
            device_id_type=pl.DeviceIdType.MESH,
        )

    def chain_copy(turn):
        return pltpu.make_async_remote_copy(
            src_ref=chain_out.at[turn],
            dst_ref=chain_in.at[turn],
            send_sem=chain_send.at[turn],
            recv_sem=chain_recv.at[turn],
            device_id={"seq": above},
            device_id_type=pl.DeviceIdType.MESH,
        )

    def swap_copy(turn):
        return pltpu.make_async_remote_copy(
            src_ref=chain_in.at[turn],
            dst_ref=swap_in.at[turn],
            send_sem=swap_send.at[turn],
            recv_sem=swap_recv.at[turn],
            device_id={"seq": partners[0]},
            device_id_type=pl.DeviceIdType.MESH,
        )

    host = jnp.where(pair == 1, below, partners[-1])
    guest = jnp.where(pair == 0, above, partners[-1])

    def served(turn):
        return (turn >= chunks - serve) & (turn < chunks) if serve else False

    def served_turn(index):
        return chunks - serve + index

    def served_index(turn):
        return turn - (chunks - serve)

    def withheld(bit, turn):
        return served(turn) & (pair == bit - 1)

    def ask_copy(index):
        return pltpu.make_async_remote_copy(
            src_ref=q_hbm.at[:, head_columns((place(served_turn(index), side) + 1) * per_chunk - 1)],
            dst_ref=guest_q.at[index],
            send_sem=ask_send.at[index],
            recv_sem=ask_recv.at[index],
            device_id={"seq": host},
            device_id_type=pl.DeviceIdType.MESH,
        )

    def answer_copies(index):
        return [
            pltpu.make_async_remote_copy(
                src_ref=source.at[index],
                dst_ref=target.at[index],
                send_sem=answer_send.at[index, part],
                recv_sem=answer_recv.at[index, part],
                device_id={"seq": guest},
                device_id_type=pl.DeviceIdType.MESH,
            )
            for part, (source, target) in enumerate(((served_out, served_in), (stats_out, stats_in)))
        ]

    loads = [
        pltpu.make_async_copy(source, target, load_sem.at[index])
        for index, (source, target) in enumerate(
            ((k_hbm, k_ref), (v_hbm, v_ref), (q_hbm, q_ref), (len_hbm, len_ref), (scale_hbm, scale_ref))
        )
    ]
    for load in loads:
        load.start()
    barrier = pltpu.get_barrier_semaphore()
    greeted = partners + [above, below]
    for other in greeted:
        pl.semaphore_signal(
            barrier, inc=1, device_id={"seq": other}, device_id_type=pl.DeviceIdType.MESH
        )
    pl.semaphore_wait(barrier, len(greeted))

    def for_each_far(turn, action):
        if serve:
            for part in range(2):
                for bit in range(1, levels):
                    pl.when(jnp.logical_not(withheld(bit, turn)))(lambda bit=bit: action(block_copy(bit, turn, part, side)))
                    pl.when(withheld(bit, turn))(lambda bit=bit: action(block_copy(bit, turn, part, side, per_chunk - 1)))
            return
        for bit in range(1, levels):
            def whole(bit=bit):
                for part in range(2):
                    action(block_copy(bit, turn, part, side))

            def less(bit=bit):
                for part in range(2):
                    action(block_copy(bit, turn, part, side, per_chunk - 1))

            if serve:
                pl.when(jnp.logical_not(withheld(bit, turn)))(whole)
                pl.when(withheld(bit, turn))(less)
            else:
                whole()

    def send_far(turn):
        for_each_far(turn, lambda copy: copy.start())

    def send_near(turn, _):
        for part in range(2):
            block_copy(0, turn, part, 1 - side).start()
        return 0

    def sent_by(turn):
        more = jnp.maximum(turn - delay(pair) - calm, 0)
        return jnp.minimum(window + turn + 1 + more, chunks)

    if serve:
        @pl.when(lax.rem(pair, 2) == 1)
        def _():
            for index in range(serve):
                ask_copy(index).start()

    lax.fori_loop(0, sent_by(-1), lambda turn, _: (send_far(turn), 0)[1], 0)
    lax.fori_loop(0, chunks, send_near, 0)

    row_ids = lax.broadcasted_iota(jnp.int32, (rows, rows), 0)
    column_ids = lax.broadcasted_iota(jnp.int32, (rows, rows), 1)
    live_rows = lax.broadcasted_iota(jnp.int32, (rows, width), 0)
    root = 1.0 / math.sqrt(width)

    for load in loads:
        load.wait()
    lengths = [len_ref[me]] + [len_ref[partner] for partner in partners]

    def key_value_sum(keys, values, length):
        mapped = jnp.where(live_rows < length, feature(keys.astype(jnp.float32)), 0.0)
        return sum(
            lax.dot_general(
                term, values, (((0,), (0,)), ((), ())), preferred_element_type=jnp.float32
            )
            for term in two_terms(mapped)
        )

    def piece(queries, keys, values, length, causal):
        weights, peak, total = weigh(queries, keys, length, causal)
        return jnp.dot(weights, values, preferred_element_type=jnp.float32), peak, total

    def weigh(queries, keys, length, causal):
        scores = root * lax.dot_general(
            queries, keys, (((1,), (1,)), ((), ())), preferred_element_type=jnp.float32
        )
        allowed = column_ids < length
        if causal:
            allowed = allowed & (column_ids <= row_ids)
        peak = jnp.max(jnp.where(allowed, scores, -jnp.inf), axis=1, keepdims=True)
        weights = jnp.where(allowed, jnp.exp(scores - peak), 0.0).astype(jnp.bfloat16)
        total = jnp.sum(weights.astype(jnp.float32), axis=1, keepdims=True)
        return weights, peak, total

    def merge(pieces):
        top = functools.reduce(jnp.maximum, [peak for _, peak, _ in pieces])
        numerator, denominator = 0.0, 0.0
        for part, peak, total in pieces:
            factor = jnp.exp(peak - top)
            numerator = numerator + factor * part
            denominator = denominator + factor * total
        return numerator / denominator

    def attend(turn, finishing, asked):
        chunk = place(turn, side)
        cuts = [head_columns(chunk * per_chunk + offset) for offset in range(per_chunk)]
        pieces = [
            [
                piece(q_ref[:, cut], k_ref[:, cut], v_ref[:, cut], lengths[0], True),
                piece(q_ref[:, cut], far[0, 0, :, cut], far[0, 1, :, cut], lengths[1], False),
            ]
            for cut in cuts
        ]
        if asked:
            full, cut_short = jnp.where(pair == 1, 2, 1), jnp.where(pair == 1, 1, 2)
            sources = [
                (full, jnp.where(pair == 1, lengths[3], lengths[2]), per_chunk),
                (cut_short, jnp.where(pair == 1, lengths[2], lengths[3]), per_chunk - 1),
            ]
            index = served_index(turn)
            for copy in answer_copies(index):
                copy.wait_recv()
            columns_of = jnp.tile(stats_in[index], (rows // 8, 1)).T
            pieces[-1].append((served_in[index].astype(jnp.float32), columns_of[:, :1], columns_of[:, 1:2]))
        else:
            sources = [(bit, lengths[1 + bit], per_chunk) for bit in range(1, levels)]
        heavy = []
        for bit, extent, count in sources:
            block_copy(bit, turn, 0, side, count).wait_recv()
            heavy.append([weigh(q_ref[:, cut], far[bit, 0, :, cut], extent, False) for cut in cuts[:count]])
        for (bit, extent, count), weighed in zip(sources, heavy):
            block_copy(bit, turn, 1, side, count).wait_recv()
            for cut, found, (weights, peak, total) in zip(cuts, pieces, weighed):
                numerator = jnp.dot(weights, far[bit, 1, :, cut], preferred_element_type=jnp.float32)
                found.append((numerator, peak, total))
        for cut, found in zip(cuts, pieces):
            attention = merge(found)
            if finishing:
                out_ref[:, cut] = (attention + acc[:, cut]).astype(out_ref.dtype)
            else:
                acc[:, cut] = attention

    def answer(index):
        ask_copy(index).wait_recv()
        cut = head_columns((place(served_turn(index), side) + 1) * per_chunk - 1)
        numerator, peak, total = piece(guest_q[index], k_ref[:, cut], v_ref[:, cut], lengths[0], False)
        served_out[index] = numerator.astype(jnp.bfloat16)
        lanes = jnp.where(column_ids == 0, peak, total)
        stats_out[index] = lanes.T[:8]
        for copy in answer_copies(index):
            copy.start()

    def add_linear(head, prefix, finishing):
        cut = head_columns(head)
        near = jnp.where(side > 0, near_sums[head], 0.0)
        prefix = jnp.where(pair > 0, prefix.astype(jnp.float32), 0.0) + near
        coarse, fine = two_terms(feature(q_ref[:, cut].astype(jnp.float32)))
        sums, rest = two_terms(prefix)
        linear = sum(
            jnp.dot(left, right, preferred_element_type=jnp.float32)
            for left, right in ((coarse, sums), (fine, sums), (coarse, rest))
        )
        gain = scale_ref[head] / (width * math.sqrt(rows * blocks))
        linear = gain * linear
        if finishing:
            out_ref[:, cut] = (acc[:, cut] + linear).astype(out_ref.dtype)
        else:
            acc[:, cut] = linear

    def prepare(step):
        for part in range(2):
            block_copy(0, step, part, side).wait_recv()
        chunk = place(step, side)

        @pl.when((step < half) | (side > 0))
        def _():
            for offset in range(per_chunk):
                head = chunk * per_chunk + offset
                cut = head_columns(head)
                near_sums[head] = key_value_sum(far[0, 0, :, cut], far[0, 1, :, cut], lengths[1])

        @pl.when((step < half) & (pair < pairs - 1))
        def _():
            for offset in range(per_chunk):
                cut = head_columns(chunk * per_chunk + offset)
                own_sums[step * per_chunk + offset] = key_value_sum(k_ref[:, cut], v_ref[:, cut], lengths[0])

    def pass_on(link):
        first = place(link, side) * per_chunk

        @pl.when(pair > 0)
        def _():
            chain_copy(link).wait_recv()

        @pl.when(pair < pairs - 1)
        def _():
            for offset in range(per_chunk):
                both = own_sums[link * per_chunk + offset] + near_sums[first + offset]
                before = jnp.where(pair > 0, chain_in[link, offset].astype(jnp.float32), 0.0)
                chain_out[link, offset] = (both + before).astype(jnp.bfloat16)
            chain_copy(link).start()

        @pl.when(pair > 0)
        def _():
            swap_copy(link).start()

    def finish_linear(late):
        @pl.when(pair > 0)
        def _():
            swap_copy(late).wait_recv()

        for offset in range(per_chunk):
            add_linear(place(late, side) * per_chunk + offset, chain_in[late, offset], True)

        def other(finishing):
            for offset in range(per_chunk):
                add_linear(place(late, 1 - side) * per_chunk + offset, swap_in[late, offset], finishing)

        if joined:
            pl.when(late < half - 1)(lambda: other(True))
            pl.when(late == half - 1)(lambda: other(False))
        else:
            other(True)

    def steps(first, limit, action):
        for offset in range(STEPS):
            step = first * STEPS + offset
            pl.when((step >= 0) & (step < limit))(functools.partial(action, step))

    def one_turn(turn, _):
        steps(turn, chunks, prepare)
        steps(turn - delay(pair), half, pass_on)
        lax.fori_loop(sent_by(turn - 1), sent_by(turn), lambda chunk, _: (send_far(chunk), 0)[1], 0)
        steps(turn - linear_lag, half, finish_linear)

        if serve:
            @pl.when((pair < pairs // 2) & (turn > 0) & (turn <= serve))
            def _():
                answer(turn - 1)

        asking = served(turn) & (lax.rem(pair, 2) == 1)
        inside = turn < (chunks - 1 if joined else chunks)
        if serve:
            pl.when(inside & jnp.logical_not(asking))(lambda: attend(turn, False, False))
            pl.when(inside & asking)(lambda: attend(turn, False, True))
        else:
            pl.when(inside)(lambda: attend(turn, False, False))
        if joined:
            last = turn == chunks - 1
            if serve:
                pl.when(last & jnp.logical_not(asking))(lambda: attend(turn, True, False))
                pl.when(last & asking)(lambda: attend(turn, True, True))
            else:
                pl.when(last)(lambda: attend(turn, True, False))

        return 0

    @pl.when(pair == 0)
    def _():
        def clear(turn, _):
            chain_in[turn] = jnp.zeros_like(chain_in[turn])
            swap_in[turn] = jnp.zeros_like(swap_in[turn])
            return 0

        lax.fori_loop(0, half, clear, 0)

    lax.fori_loop(0, turns, one_turn, 0)

    def finish(turn, _):
        for part in range(2):
            block_copy(0, turn, part, 1 - side).wait_send()
        for_each_far(turn, lambda copy: copy.wait_send())
        return 0

    lax.fori_loop(0, chunks, finish, 0)

    def finish_chain(turn, _):
        @pl.when(pair < pairs - 1)
        def _():
            chain_copy(turn).wait_send()

        @pl.when(pair > 0)
        def _():
            swap_copy(turn).wait_send()

        return 0

    lax.fori_loop(0, half, finish_chain, 0)

    def finish_served(index, _):
        @pl.when(lax.rem(pair, 2) == 1)
        def _():
            ask_copy(index).wait_send()

        @pl.when(pair < pairs // 2)
        def _():
            for copy in answer_copies(index):
                copy.wait_send()

        return 0

    lax.fori_loop(0, serve, finish_served, 0)


def delay(pair):
    return (LAG_TIMES * pair + 1) // LAG_OVER


def shards(blocks, query_rows, key_rows, value_rows, key_len, linear_scale):
    rows, total = query_rows.shape
    heads = linear_scale.shape[0]
    width = total // heads
    levels = blocks.bit_length() - 1
    chunks = heads // HEADS_PER_CHUNK
    half = chunks // 2
    serve = SERVED if blocks == 8 else 0
    guests = max(serve, 1)
    vmem = pl.BlockSpec(memory_space=pltpu.VMEM)
    hbm = pl.BlockSpec(memory_space=pltpu.HBM)
    piece = (half, HEADS_PER_CHUNK, width, width)
    dma = pltpu.SemaphoreType.DMA
    return pl.pallas_call(
        functools.partial(kernel, blocks, heads, width, HEADS_PER_CHUNK, WINDOW, CALM, delay, serve),
        out_shape=jax.ShapeDtypeStruct((rows, total), query_rows.dtype),
        in_specs=[hbm, hbm, hbm, hbm, hbm],
        out_specs=vmem,
        scratch_shapes=[
            pltpu.SMEM((blocks,), jnp.int32),
            pltpu.SMEM((heads,), jnp.float32),
            pltpu.VMEM((rows, total), jnp.bfloat16),
            pltpu.VMEM((rows, total), jnp.bfloat16),
            pltpu.VMEM((rows, total), jnp.bfloat16),
            dma((5,)),
            pltpu.VMEM((levels, 2, rows, total), jnp.bfloat16),
            pltpu.VMEM((rows, total), jnp.float32),
            pltpu.VMEM((heads // 2, width, width), jnp.float32),
            pltpu.VMEM((heads, width, width), jnp.float32),
            pltpu.VMEM(piece, jnp.bfloat16),
            pltpu.VMEM(piece, jnp.bfloat16),
            pltpu.VMEM(piece, jnp.bfloat16),
            dma((levels, chunks, 2)),
            dma((levels, chunks, 2)),
            dma((half,)),
            dma((half,)),
            dma((half,)),
            dma((half,)),
            pltpu.VMEM((guests, rows, width), jnp.bfloat16),
            pltpu.VMEM((guests, rows, width), jnp.bfloat16),
            pltpu.VMEM((guests, rows, width), jnp.bfloat16),
            pltpu.VMEM((guests, 8, rows), jnp.float32),
            pltpu.VMEM((guests, 8, rows), jnp.float32),
            dma((guests,)),
            dma((guests,)),
            dma((guests, 2)),
            dma((guests, 2)),
        ],
        compiler_params=pltpu.CompilerParams(
            collective_id=0, has_side_effects=True, vmem_limit_bytes=55000000
        ),
        name="butterfly",
    )(
        pltpu.with_memory_space_constraint(key_len, pltpu.HBM),
        pltpu.with_memory_space_constraint(linear_scale, pltpu.HBM),
        query_rows, key_rows, value_rows,
    )


def solution(mesh):
    return jax.shard_map(
        functools.partial(shards, mesh.shape["seq"]),
        mesh=mesh,
        in_specs=(
            P(("groups", "seq"), "head"),
            P(("groups", "seq"), "head"),
            P(("groups", "seq"), "head"),
            P("groups"),
            P("head"),
        ),
        out_specs=P(("groups", "seq"), "head"),
        check_vma=False,
    )
```

```python
import functools
import math

import jax
import jax.numpy as jnp
from jax import lax
from jax.experimental import pallas as pl
from jax.experimental.pallas import tpu as pltpu
from jax.sharding import PartitionSpec as P

HEADS_PER_CHUNK = 2
WINDOW = 2
STEPS = 2
CALM = 3
SERVED = 5
LAG_TIMES = 6
LAG_OVER = 3


def feature(inputs):
    return jnp.where(inputs > 0.0, inputs + 1.0, jnp.exp(jnp.minimum(inputs, 0.0)))


def two_terms(wide):
    coarse = wide.astype(jnp.bfloat16)
    return coarse, (wide - coarse.astype(jnp.float32)).astype(jnp.bfloat16)


def kernel(
    blocks, heads, width, per_chunk, window, calm, delay, serve,
    len_hbm, scale_hbm, q_hbm, k_hbm, v_hbm, out_ref,
    len_ref, scale_ref, q_ref, k_ref, v_ref, load_sem, far, acc, own_sums, near_sums, chain_out, chain_in, swap_in,
    send_sem, recv_sem, near_recv, chain_send, chain_recv, swap_send, swap_recv,
    guest_q, served_out, served_in, stats_out, stats_in, ask_send, ask_recv, answer_send, answer_recv,
):
    rows = q_ref.shape[0]
    levels = blocks.bit_length() - 1
    chunks = heads // per_chunk
    half = chunks // 2
    pairs = blocks // 2
    span = per_chunk * width
    step_count = STEPS if half % STEPS == 0 else 1
    rounds = half // step_count
    linear_lag = max(chunks - rounds, delay(pairs - 1) + 1)
    joined = linear_lag + rounds == chunks
    turns = linear_lag + rounds

    me = lax.axis_index("seq")
    side = lax.rem(me, 2)
    pair = me // 2
    partners = [me + (1 - 2 * lax.rem(me // (1 << bit), 2)) * (1 << bit) for bit in range(levels)]
    above = lax.rem(me + 2, blocks)
    below = lax.rem(me + blocks - 2, blocks)

    def place(turn, which):
        return lax.rem(turn + half * which, chunks)

    def columns(chunk):
        return pl.ds(pl.multiple_of(chunk * span, span), span)

    def head_columns(head):
        return pl.ds(pl.multiple_of(head * width, width), width)

    def slot(turn, part):
        return jnp.where(turn == chunks - 1, chunks, turn) if joined and part else turn

    def arrival(place_in_far, received):
        return pltpu.make_async_remote_copy(
            src_ref=place_in_far,
            dst_ref=place_in_far,
            send_sem=send_sem.at[0, 0],
            recv_sem=received,
            device_id={"seq": partners[0]},
            device_id_type=pl.DeviceIdType.MESH,
        )

    def near_arrival(group):
        start = place(group * step_count, side) * span
        cut = pl.ds(pl.multiple_of(start, span), step_count * span)
        return arrival(far.at[0, :, :, cut], near_recv.at[group])

    def far_arrival(bit, turn, count):
        cut = pl.ds(pl.multiple_of(place(turn, side) * span, span), count * width)
        return arrival(far.at[bit, :, :, cut], recv_sem.at[bit - 1, turn])

    def departure(source, sent):
        return pltpu.make_async_remote_copy(
            src_ref=source,
            dst_ref=source,
            send_sem=sent,
            recv_sem=near_recv.at[0],
            device_id={"seq": partners[0]},
            device_id_type=pl.DeviceIdType.MESH,
        )

    def block_copy(bit, turn, part, which, heads_sent=per_chunk):
        source = k_hbm if part == 0 else v_hbm
        cut = pl.ds(pl.multiple_of(place(turn, which) * span, span), heads_sent * width)
        return pltpu.make_async_remote_copy(
            src_ref=source.at[:, cut],
            dst_ref=far.at[bit, part, :, cut],
            send_sem=send_sem.at[bit, part],
            recv_sem=near_recv.at[turn // step_count] if isinstance(bit, int) and bit == 0 else recv_sem.at[bit - 1, slot(turn, part)],
            device_id={"seq": partners[bit] if isinstance(bit, int) else partners[1]},
            device_id_type=pl.DeviceIdType.MESH,
        )

    def in_round(number):
        return pl.ds(number * step_count, step_count)

    def chain_copy(number):
        return pltpu.make_async_remote_copy(
            src_ref=chain_out.at[in_round(number)],
            dst_ref=chain_in.at[in_round(number)],
            send_sem=chain_send.at[0],
            recv_sem=chain_recv.at[number],
            device_id={"seq": above},
            device_id_type=pl.DeviceIdType.MESH,
        )

    def swap_copy(number):
        return pltpu.make_async_remote_copy(
            src_ref=chain_in.at[in_round(number)],
            dst_ref=swap_in.at[in_round(number)],
            send_sem=swap_send.at[0],
            recv_sem=swap_recv.at[number],
            device_id={"seq": partners[0]},
            device_id_type=pl.DeviceIdType.MESH,
        )

    host = jnp.where(pair == 1, below, partners[-1])
    guest = jnp.where(pair == 0, above, partners[-1])

    def served(turn):
        return (turn >= chunks - serve) & (turn < chunks) if serve else False

    def served_turn(index):
        return chunks - serve + index

    def served_index(turn):
        return turn - (chunks - serve)

    def withheld(bit, turn):
        return served(turn) & (pair == bit - 1)

    def ask_copy(index):
        return pltpu.make_async_remote_copy(
            src_ref=q_hbm.at[:, head_columns((place(served_turn(index), side) + 1) * per_chunk - 1)],
            dst_ref=guest_q.at[index],
            send_sem=ask_send.at[0],
            recv_sem=ask_recv.at[0],
            device_id={"seq": host},
            device_id_type=pl.DeviceIdType.MESH,
        )

    def answer_copies(index):
        return [
            pltpu.make_async_remote_copy(
                src_ref=source.at[index],
                dst_ref=target.at[index],
                send_sem=answer_send.at[part],
                recv_sem=answer_recv.at[index, part],
                device_id={"seq": guest},
                device_id_type=pl.DeviceIdType.MESH,
            )
            for part, (source, target) in enumerate(((served_out, served_in), (stats_out, stats_in)))
        ]

    loads = [
        pltpu.make_async_copy(source, target, load_sem.at[index])
        for index, (source, target) in enumerate(
            ((k_hbm, k_ref), (v_hbm, v_ref), (q_hbm, q_ref), (len_hbm, len_ref), (scale_hbm, scale_ref))
        )
    ]
    barrier = pltpu.get_barrier_semaphore()
    greeted = partners + [above, below]
    for other in greeted:
        pl.semaphore_signal(
            barrier, inc=1, device_id={"seq": other}, device_id_type=pl.DeviceIdType.MESH
        )
    for load in loads:
        load.start()
    pl.semaphore_wait(barrier, len(greeted))

    def for_each_far(turn, action):
        if serve:
            for part in range(2):
                for bit in range(1, levels):
                    pl.when(jnp.logical_not(withheld(bit, turn)))(lambda bit=bit: action(block_copy(bit, turn, part, side)))
                    pl.when(withheld(bit, turn))(lambda bit=bit: action(block_copy(bit, turn, part, side, per_chunk - 1)))
            return
        for bit in range(1, levels):
            def whole(bit=bit):
                for part in range(2):
                    action(block_copy(bit, turn, part, side))

            def less(bit=bit):
                for part in range(2):
                    action(block_copy(bit, turn, part, side, per_chunk - 1))

            if serve:
                pl.when(jnp.logical_not(withheld(bit, turn)))(whole)
                pl.when(withheld(bit, turn))(less)
            else:
                whole()

    def send_far(turn):
        for_each_far(turn, lambda copy: copy.start())

    def send_near(turn, _):
        for part in range(2):
            block_copy(0, turn, part, 1 - side).start()
        return 0

    def sent_by(turn):
        more = jnp.maximum(turn - delay(pair) - calm, 0)
        return jnp.minimum(window + turn + 1 + more, chunks)

    if serve:
        @pl.when(lax.rem(pair, 2) == 1)
        def _():
            for index in range(serve):
                ask_copy(index).start()

    lax.fori_loop(0, sent_by(-1), lambda turn, _: (send_far(turn), 0)[1], 0)
    lax.fori_loop(0, chunks, send_near, 0)

    row_ids = lax.broadcasted_iota(jnp.int32, (rows, rows), 0)
    column_ids = lax.broadcasted_iota(jnp.int32, (rows, rows), 1)
    live_rows = lax.broadcasted_iota(jnp.int32, (rows, width), 0)
    root = 1.0 / math.sqrt(width)

    for load in loads:
        load.wait()
    lengths = [len_ref[me]] + [len_ref[partner] for partner in partners]

    def key_value_sum(keys, values, length):
        mapped = jnp.where(live_rows < length, feature(keys.astype(jnp.float32)), 0.0)
        return sum(
            lax.dot_general(
                term, values, (((0,), (0,)), ((), ())), preferred_element_type=jnp.float32
            )
            for term in two_terms(mapped)
        )

    def piece(queries, keys, values, length, causal):
        weights, peak, total = weigh(queries, keys, length, causal)
        return jnp.dot(weights, values, preferred_element_type=jnp.float32), peak, total

    def weigh(queries, keys, length, causal):
        scores = root * lax.dot_general(
            queries, keys, (((1,), (1,)), ((), ())), preferred_element_type=jnp.float32
        )
        allowed = column_ids < length
        if causal:
            allowed = allowed & (column_ids <= row_ids)
        peak = jnp.max(jnp.where(allowed, scores, -jnp.inf), axis=1, keepdims=True)
        weights = jnp.where(allowed, jnp.exp(scores - peak), 0.0).astype(jnp.bfloat16)
        total = jnp.sum(weights.astype(jnp.float32), axis=1, keepdims=True)
        return weights, peak, total

    def merge(pieces):
        top = functools.reduce(jnp.maximum, [peak for _, peak, _ in pieces])
        numerator, denominator = 0.0, 0.0
        for part, peak, total in pieces:
            factor = jnp.exp(peak - top)
            numerator = numerator + factor * part
            denominator = denominator + factor * total
        return numerator / denominator

    def attend(turn, finishing, asked):
        chunk = place(turn, side)
        cuts = [head_columns(chunk * per_chunk + offset) for offset in range(per_chunk)]
        pieces = [
            [
                piece(q_ref[:, cut], k_ref[:, cut], v_ref[:, cut], lengths[0], True),
                piece(q_ref[:, cut], far[0, 0, :, cut], far[0, 1, :, cut], lengths[1], False),
            ]
            for cut in cuts
        ]
        if asked:
            full, cut_short = jnp.where(pair == 1, 2, 1), jnp.where(pair == 1, 1, 2)
            sources = [
                (full, jnp.where(pair == 1, lengths[3], lengths[2]), per_chunk),
                (cut_short, jnp.where(pair == 1, lengths[2], lengths[3]), per_chunk - 1),
            ]
            index = served_index(turn)
            for copy in answer_copies(index):
                copy.wait_recv()
            columns_of = jnp.tile(stats_in[index], (rows // 8, 1)).T
            pieces[-1].append((served_in[index].astype(jnp.float32), columns_of[:, :1], columns_of[:, 1:2]))
        else:
            sources = [(bit, lengths[1 + bit], per_chunk) for bit in range(1, levels)]
        if finishing:
            heavy = []
            for bit, extent, count in sources:
                block_copy(bit, turn, 0, side, count).wait_recv()
                heavy.append([weigh(q_ref[:, cut], far[bit, 0, :, cut], extent, False) for cut in cuts[:count]])
            for (bit, extent, count), weighed in zip(sources, heavy):
                block_copy(bit, turn, 1, side, count).wait_recv()
                for cut, found, (weights, peak, total) in zip(cuts, pieces, weighed):
                    numerator = jnp.dot(weights, far[bit, 1, :, cut], preferred_element_type=jnp.float32)
                    found.append((numerator, peak, total))
        else:
            for bit, extent, count in sources:
                far_arrival(bit, turn, count).wait_recv()
                for cut, found in list(zip(cuts, pieces))[:count]:
                    found.append(piece(q_ref[:, cut], far[bit, 0, :, cut], far[bit, 1, :, cut], extent, False))
        for cut, found in zip(cuts, pieces):
            attention = merge(found)
            if finishing:
                out_ref[:, cut] = (attention + acc[:, cut]).astype(out_ref.dtype)
            else:
                acc[:, cut] = attention

    def answer(index):
        @pl.when(index == 0)
        def _():
            arrival(guest_q, ask_recv.at[0]).wait_recv()

        cut = head_columns((place(served_turn(index), side) + 1) * per_chunk - 1)
        numerator, peak, total = piece(guest_q[index], k_ref[:, cut], v_ref[:, cut], lengths[0], False)
        served_out[index] = numerator.astype(jnp.bfloat16)
        lanes = jnp.where(column_ids == 0, peak, total)
        stats_out[index] = lanes.T[:8]
        for copy in answer_copies(index):
            copy.start()

    def add_linear(head, prefix, finishing):
        cut = head_columns(head)
        near = jnp.where(side > 0, near_sums[head], 0.0)
        prefix = jnp.where(pair > 0, prefix.astype(jnp.float32), 0.0) + near
        coarse, fine = two_terms(feature(q_ref[:, cut].astype(jnp.float32)))
        sums, rest = two_terms(prefix)
        linear = sum(
            jnp.dot(left, right, preferred_element_type=jnp.float32)
            for left, right in ((coarse, sums), (fine, sums), (coarse, rest))
        )
        gain = scale_ref[head] / (width * math.sqrt(rows * blocks))
        linear = gain * linear
        if finishing:
            out_ref[:, cut] = (acc[:, cut] + linear).astype(out_ref.dtype)
        else:
            acc[:, cut] = linear

    def prepare(step):
        chunk = place(step, side)

        @pl.when((step < half) | (side > 0))
        def _():
            for offset in range(per_chunk):
                head = chunk * per_chunk + offset
                cut = head_columns(head)
                near_sums[head] = key_value_sum(far[0, 0, :, cut], far[0, 1, :, cut], lengths[1])

        @pl.when((step < half) & (pair < pairs - 1))
        def _():
            for offset in range(per_chunk):
                cut = head_columns(chunk * per_chunk + offset)
                own_sums[step * per_chunk + offset] = key_value_sum(k_ref[:, cut], v_ref[:, cut], lengths[0])

    def prepare_group(group):
        near_arrival(group).wait_recv()
        for offset in range(step_count):
            prepare(group * step_count + offset)

    def pass_on(number):
        @pl.when(pair > 0)
        def _():
            chain_copy(number).wait_recv()

        @pl.when(pair < pairs - 1)
        def _():
            for part in range(step_count):
                link = number * step_count + part
                first = place(link, side) * per_chunk
                for offset in range(per_chunk):
                    both = own_sums[link * per_chunk + offset] + near_sums[first + offset]
                    before = jnp.where(pair > 0, chain_in[link, offset].astype(jnp.float32), 0.0)
                    chain_out[link, offset] = (both + before).astype(jnp.bfloat16)
            chain_copy(number).start()

        @pl.when(pair > 0)
        def _():
            swap_copy(number).start()

    def linear_round(number):
        @pl.when(pair > 0)
        def _():
            swap_copy(number).wait_recv()

        for part in range(step_count):
            finish_linear(number * step_count + part)

    def finish_linear(late):
        for offset in range(per_chunk):
            add_linear(place(late, side) * per_chunk + offset, chain_in[late, offset], True)

        def other(finishing):
            for offset in range(per_chunk):
                add_linear(place(late, 1 - side) * per_chunk + offset, swap_in[late, offset], finishing)

        if joined:
            pl.when(late < half - 1)(lambda: other(True))
            pl.when(late == half - 1)(lambda: other(False))
        else:
            other(True)

    def one_turn(turn, _):
        pl.when(turn < chunks // step_count)(lambda: prepare_group(turn))
        number = turn - delay(pair)
        pl.when((number >= 0) & (number < rounds))(lambda: pass_on(number))
        lax.fori_loop(sent_by(turn - 1), sent_by(turn), lambda chunk, _: (send_far(chunk), 0)[1], 0)
        pl.when((turn >= linear_lag) & (turn - linear_lag < rounds))(lambda: linear_round(turn - linear_lag))

        if serve:
            @pl.when((pair < pairs // 2) & (turn > 0) & (turn <= serve))
            def _():
                answer(turn - 1)

        asking = served(turn) & (lax.rem(pair, 2) == 1)
        inside = turn < (chunks - 1 if joined else chunks)
        if serve:
            pl.when(inside & jnp.logical_not(asking))(lambda: attend(turn, False, False))
            pl.when(inside & asking)(lambda: attend(turn, False, True))
        else:
            pl.when(inside)(lambda: attend(turn, False, False))
        if joined:
            last = turn == chunks - 1
            if serve:
                pl.when(last & jnp.logical_not(asking))(lambda: attend(turn, True, False))
                pl.when(last & asking)(lambda: attend(turn, True, True))
            else:
                pl.when(last)(lambda: attend(turn, True, False))

        return 0

    @pl.when(pair == 0)
    def _():
        def clear(turn, _):
            chain_in[turn] = jnp.zeros_like(chain_in[turn])
            swap_in[turn] = jnp.zeros_like(swap_in[turn])
            return 0

        lax.fori_loop(0, half, clear, 0)

    lax.fori_loop(0, turns, one_turn, 0)

    for part, source in enumerate((k_hbm, v_hbm)):
        departure(source, send_sem.at[0, part]).wait_send()
        for bit in range(1, levels):
            if serve:
                pl.when(pair != bit - 1)(departure(source, send_sem.at[bit, part]).wait_send)
                some = source.at[:, :(heads - serve) * width]
                pl.when(pair == bit - 1)(departure(some, send_sem.at[bit, part]).wait_send)
            else:
                departure(source, send_sem.at[bit, part]).wait_send()

    pl.when(pair < pairs - 1)(departure(chain_out, chain_send.at[0]).wait_send)
    pl.when(pair > 0)(departure(chain_in, swap_send.at[0]).wait_send)

    if serve:
        @pl.when(lax.rem(pair, 2) == 1)
        def _():
            departure(guest_q, ask_send.at[0]).wait_send()

        @pl.when(pair < pairs // 2)
        def _():
            departure(served_out, answer_send.at[0]).wait_send()
            departure(stats_out, answer_send.at[1]).wait_send()


def delay(pair):
    return (LAG_TIMES * pair + 1) // LAG_OVER


def shards(blocks, query_rows, key_rows, value_rows, key_len, linear_scale):
    rows, total = query_rows.shape
    heads = linear_scale.shape[0]
    width = total // heads
    levels = blocks.bit_length() - 1
    chunks = heads // HEADS_PER_CHUNK
    half = chunks // 2
    step_count = STEPS if half % STEPS == 0 else 1
    serve = SERVED if blocks == 8 else 0
    guests = max(serve, 1)
    vmem = pl.BlockSpec(memory_space=pltpu.VMEM)
    hbm = pl.BlockSpec(memory_space=pltpu.HBM)
    piece = (half, HEADS_PER_CHUNK, width, width)
    dma = pltpu.SemaphoreType.DMA
    return pl.pallas_call(
        functools.partial(kernel, blocks, heads, width, HEADS_PER_CHUNK, WINDOW, CALM, delay, serve),
        out_shape=jax.ShapeDtypeStruct((rows, total), query_rows.dtype),
        in_specs=[hbm, hbm, hbm, hbm, hbm],
        out_specs=vmem,
        scratch_shapes=[
            pltpu.SMEM((blocks,), jnp.int32),
            pltpu.SMEM((heads,), jnp.float32),
            pltpu.VMEM((rows, total), jnp.bfloat16),
            pltpu.VMEM((rows, total), jnp.bfloat16),
            pltpu.VMEM((rows, total), jnp.bfloat16),
            dma((5,)),
            pltpu.VMEM((levels, 2, rows, total), jnp.bfloat16),
            pltpu.VMEM((rows, total), jnp.float32),
            pltpu.VMEM((heads // 2, width, width), jnp.float32),
            pltpu.VMEM((heads, width, width), jnp.float32),
            pltpu.VMEM(piece, jnp.bfloat16),
            pltpu.VMEM(piece, jnp.bfloat16),
            pltpu.VMEM(piece, jnp.bfloat16),
            dma((levels, 2)),
            dma((levels - 1, chunks + 1)),
            dma((chunks // step_count,)),
            dma((1,)),
            dma((half // step_count,)),
            dma((1,)),
            dma((half // step_count,)),
            pltpu.VMEM((guests, rows, width), jnp.bfloat16),
            pltpu.VMEM((guests, rows, width), jnp.bfloat16),
            pltpu.VMEM((guests, rows, width), jnp.bfloat16),
            pltpu.VMEM((guests, 8, rows), jnp.float32),
            pltpu.VMEM((guests, 8, rows), jnp.float32),
            dma((1,)),
            dma((1,)),
            dma((2,)),
            dma((guests, 2)),
        ],
        compiler_params=pltpu.CompilerParams(
            collective_id=0, has_side_effects=True, vmem_limit_bytes=55000000
        ),
        name="butterfly",
    )(
        pltpu.with_memory_space_constraint(key_len, pltpu.HBM),
        pltpu.with_memory_space_constraint(linear_scale, pltpu.HBM),
        query_rows, key_rows, value_rows,
    )


def solution(mesh):
    return jax.shard_map(
        functools.partial(shards, mesh.shape["seq"]),
        mesh=mesh,
        in_specs=(
            P(("groups", "seq"), "head"),
            P(("groups", "seq"), "head"),
            P(("groups", "seq"), "head"),
            P("groups"),
            P("head"),
        ),
        out_specs=P(("groups", "seq"), "head"),
        check_vma=False,
    )
```

```python
import functools
import math

import jax
import jax.numpy as jnp
from jax import lax
from jax.experimental import pallas as pl
from jax.experimental.pallas import tpu as pltpu
from jax.sharding import PartitionSpec as P

HEADS_PER_CHUNK = 2
WINDOW = 3
STEPS = 2
CALM = 3
SERVED = 5
LAG_TIMES = 6
LAG_OVER = 3


def feature(inputs):
    return jnp.where(inputs > 0.0, inputs + 1.0, jnp.exp(jnp.minimum(inputs, 0.0)))


def two_terms(wide):
    coarse = wide.astype(jnp.bfloat16)
    return coarse, (wide - coarse.astype(jnp.float32)).astype(jnp.bfloat16)


def kernel(
    blocks, heads, width, per_chunk, window, calm, delay, serve,
    len_hbm, scale_hbm, q_hbm, k_hbm, v_hbm, out_ref,
    len_ref, scale_ref, q_ref, k_ref, v_ref, load_sem, far, acc, own_sums, near_sums, chain_out, chain_in, swap_in,
    send_sem, recv_sem, near_recv, chain_send, chain_recv, swap_send, swap_recv,
    guest_q, served_out, served_in, stats_out, stats_in, ask_send, ask_recv, answer_send, answer_recv,
):
    rows = q_ref.shape[0]
    levels = blocks.bit_length() - 1
    chunks = heads // per_chunk
    half = chunks // 2
    pairs = blocks // 2
    span = per_chunk * width
    step_count = STEPS if half % STEPS == 0 else 1
    rounds = half // step_count
    linear_lag = max(chunks - rounds, delay(pairs - 1) + 1)
    joined = linear_lag + rounds == chunks
    turns = linear_lag + rounds

    me = lax.axis_index("seq")
    side = lax.rem(me, 2)
    pair = me // 2
    partners = [me + (1 - 2 * lax.rem(me // (1 << bit), 2)) * (1 << bit) for bit in range(levels)]
    above = lax.rem(me + 2, blocks)
    below = lax.rem(me + blocks - 2, blocks)

    def place(turn, which):
        return lax.rem(turn + half * which, chunks)

    def columns(chunk):
        return pl.ds(pl.multiple_of(chunk * span, span), span)

    def head_columns(head):
        return pl.ds(pl.multiple_of(head * width, width), width)

    def slot(turn, part):
        return jnp.where(turn == chunks - 1, chunks, turn) if joined and part else turn

    def arrival(place_in_far, received):
        return pltpu.make_async_remote_copy(
            src_ref=place_in_far,
            dst_ref=place_in_far,
            send_sem=send_sem.at[0, 0],
            recv_sem=received,
            device_id={"seq": partners[0]},
            device_id_type=pl.DeviceIdType.MESH,
        )

    def near_arrival(group):
        start = place(group * step_count, side) * span
        cut = pl.ds(pl.multiple_of(start, span), step_count * span)
        return arrival(far.at[0, :, :, cut], near_recv.at[group])

    def far_arrival(bit, turn, count):
        cut = pl.ds(pl.multiple_of(place(turn, side) * span, span), count * width)
        return arrival(far.at[bit, :, :, cut], recv_sem.at[bit - 1, turn])

    def departure(source, sent):
        return pltpu.make_async_remote_copy(
            src_ref=source,
            dst_ref=source,
            send_sem=sent,
            recv_sem=near_recv.at[0],
            device_id={"seq": partners[0]},
            device_id_type=pl.DeviceIdType.MESH,
        )

    def block_copy(bit, turn, part, which, heads_sent=per_chunk):
        source = k_hbm if part == 0 else v_hbm
        cut = pl.ds(pl.multiple_of(place(turn, which) * span, span), heads_sent * width)
        return pltpu.make_async_remote_copy(
            src_ref=source.at[:, cut],
            dst_ref=far.at[bit, part, :, cut],
            send_sem=send_sem.at[bit, part],
            recv_sem=near_recv.at[turn // step_count] if isinstance(bit, int) and bit == 0 else recv_sem.at[bit - 1, slot(turn, part)],
            device_id={"seq": partners[bit] if isinstance(bit, int) else partners[1]},
            device_id_type=pl.DeviceIdType.MESH,
        )

    def in_round(number):
        return pl.ds(number * step_count, step_count)

    def chain_copy(number):
        return pltpu.make_async_remote_copy(
            src_ref=chain_out.at[in_round(number)],
            dst_ref=chain_in.at[in_round(number)],
            send_sem=chain_send.at[0],
            recv_sem=chain_recv.at[number],
            device_id={"seq": above},
            device_id_type=pl.DeviceIdType.MESH,
        )

    def swap_copy(number):
        return pltpu.make_async_remote_copy(
            src_ref=chain_in.at[in_round(number)],
            dst_ref=swap_in.at[in_round(number)],
            send_sem=swap_send.at[0],
            recv_sem=swap_recv.at[number],
            device_id={"seq": partners[0]},
            device_id_type=pl.DeviceIdType.MESH,
        )

    host = jnp.where(pair == 1, below, partners[-1])
    guest = jnp.where(pair == 0, above, partners[-1])

    def served(turn):
        return (turn >= chunks - serve) & (turn < chunks) if serve else False

    def served_turn(index):
        return chunks - serve + index

    def served_index(turn):
        return turn - (chunks - serve)

    def withheld(bit, turn):
        return served(turn) & (pair == bit - 1)

    def ask_copy(index):
        return pltpu.make_async_remote_copy(
            src_ref=q_hbm.at[:, head_columns((place(served_turn(index), side) + 1) * per_chunk - 1)],
            dst_ref=guest_q.at[index],
            send_sem=ask_send.at[0],
            recv_sem=ask_recv.at[0],
            device_id={"seq": host},
            device_id_type=pl.DeviceIdType.MESH,
        )

    def answer_copies(index):
        return [
            pltpu.make_async_remote_copy(
                src_ref=source.at[index],
                dst_ref=target.at[index],
                send_sem=answer_send.at[part],
                recv_sem=answer_recv.at[index, part],
                device_id={"seq": guest},
                device_id_type=pl.DeviceIdType.MESH,
            )
            for part, (source, target) in enumerate(((served_out, served_in), (stats_out, stats_in)))
        ]

    loads = [
        pltpu.make_async_copy(source, target, load_sem.at[index])
        for index, (source, target) in enumerate(
            ((k_hbm, k_ref), (v_hbm, v_ref), (q_hbm, q_ref), (len_hbm, len_ref), (scale_hbm, scale_ref))
        )
    ]
    barrier = pltpu.get_barrier_semaphore()
    greeted = partners + [above, below]
    for other in greeted:
        pl.semaphore_signal(
            barrier, inc=1, device_id={"seq": other}, device_id_type=pl.DeviceIdType.MESH
        )
    for load in loads:
        load.start()
    pl.semaphore_wait(barrier, len(greeted))

    def for_each_far(turn, action):
        if serve:
            for part in range(2):
                for bit in range(1, levels):
                    less = withheld(bit, turn)
                    pl.when(jnp.logical_not(less))(lambda: action(block_copy(bit, turn, part, side)))
                    pl.when(less)(lambda: action(block_copy(bit, turn, part, side, per_chunk - 1)))
            return
        for part in range(2):
            for bit in range(1, levels):
                action(block_copy(bit, turn, part, side))

    def send_far(turn):
        for_each_far(turn, lambda copy: copy.start())

    def send_near(turn, _):
        for part in range(2):
            block_copy(0, turn, part, 1 - side).start()
        return 0

    def sent_by(turn):
        more = jnp.maximum(turn - delay(pair) - calm, 0)
        return jnp.minimum(window + turn + 1 + more, chunks)

    if serve:
        @pl.when(lax.rem(pair, 2) == 1)
        def _():
            for index in range(serve):
                ask_copy(index).start()

    lax.fori_loop(0, sent_by(-1), lambda turn, _: (send_far(turn), 0)[1], 0)
    lax.fori_loop(0, chunks, send_near, 0)

    row_ids = lax.broadcasted_iota(jnp.int32, (rows, rows), 0)
    column_ids = lax.broadcasted_iota(jnp.int32, (rows, rows), 1)
    live_rows = lax.broadcasted_iota(jnp.int32, (rows, width), 0)
    root = 1.0 / math.sqrt(width)

    for load in loads:
        load.wait()
    lengths = [len_ref[me]] + [len_ref[partner] for partner in partners]

    def key_value_sum(keys, values, length):
        mapped = jnp.where(live_rows < length, feature(keys.astype(jnp.float32)), 0.0)
        return sum(
            lax.dot_general(
                term, values, (((0,), (0,)), ((), ())), preferred_element_type=jnp.float32
            )
            for term in two_terms(mapped)
        )

    def piece(queries, keys, values, length, causal):
        weights, peak, total = weigh(queries, keys, length, causal)
        return jnp.dot(weights, values, preferred_element_type=jnp.float32), peak, total

    def weigh(queries, keys, length, causal):
        scores = root * lax.dot_general(
            queries, keys, (((1,), (1,)), ((), ())), preferred_element_type=jnp.float32
        )
        allowed = column_ids < length
        if causal:
            allowed = allowed & (column_ids <= row_ids)
        peak = jnp.max(jnp.where(allowed, scores, -jnp.inf), axis=1, keepdims=True)
        weights = jnp.where(allowed, jnp.exp(scores - peak), 0.0).astype(jnp.bfloat16)
        total = jnp.sum(weights.astype(jnp.float32), axis=1, keepdims=True)
        return weights, peak, total

    def merge(pieces):
        top = functools.reduce(jnp.maximum, [peak for _, peak, _ in pieces])
        numerator, denominator = 0.0, 0.0
        for part, peak, total in pieces:
            factor = jnp.exp(peak - top)
            numerator = numerator + factor * part
            denominator = denominator + factor * total
        return numerator / denominator

    def attend(turn, finishing, asked):
        chunk = place(turn, side)
        cuts = [head_columns(chunk * per_chunk + offset) for offset in range(per_chunk)]
        pieces = [
            [
                piece(q_ref[:, cut], k_ref[:, cut], v_ref[:, cut], lengths[0], True),
                piece(q_ref[:, cut], far[0, 0, :, cut], far[0, 1, :, cut], lengths[1], False),
            ]
            for cut in cuts
        ]
        if asked:
            full, cut_short = jnp.where(pair == 1, 2, 1), jnp.where(pair == 1, 1, 2)
            sources = [
                (full, jnp.where(pair == 1, lengths[3], lengths[2]), per_chunk),
                (cut_short, jnp.where(pair == 1, lengths[2], lengths[3]), per_chunk - 1),
            ]
            index = served_index(turn)
            for copy in answer_copies(index):
                copy.wait_recv()
            columns_of = jnp.tile(stats_in[index], (rows // 8, 1)).T
            pieces[-1].append((served_in[index].astype(jnp.float32), columns_of[:, :1], columns_of[:, 1:2]))
        else:
            sources = [(bit, lengths[1 + bit], per_chunk) for bit in range(1, levels)]
        if finishing:
            heavy = []
            for bit, extent, count in sources:
                block_copy(bit, turn, 0, side, count).wait_recv()
                heavy.append([weigh(q_ref[:, cut], far[bit, 0, :, cut], extent, False) for cut in cuts[:count]])
            for (bit, extent, count), weighed in zip(sources, heavy):
                block_copy(bit, turn, 1, side, count).wait_recv()
                for cut, found, (weights, peak, total) in zip(cuts, pieces, weighed):
                    numerator = jnp.dot(weights, far[bit, 1, :, cut], preferred_element_type=jnp.float32)
                    found.append((numerator, peak, total))
        else:
            for bit, extent, count in sources:
                far_arrival(bit, turn, count).wait_recv()
                for cut, found in list(zip(cuts, pieces))[:count]:
                    found.append(piece(q_ref[:, cut], far[bit, 0, :, cut], far[bit, 1, :, cut], extent, False))
        for cut, found in zip(cuts, pieces):
            attention = merge(found)
            if finishing:
                out_ref[:, cut] = (attention + acc[:, cut]).astype(out_ref.dtype)
            else:
                acc[:, cut] = attention

    def answer(index):
        @pl.when(index == 0)
        def _():
            arrival(guest_q, ask_recv.at[0]).wait_recv()

        cut = head_columns((place(served_turn(index), side) + 1) * per_chunk - 1)
        numerator, peak, total = piece(guest_q[index], k_ref[:, cut], v_ref[:, cut], lengths[0], False)
        served_out[index] = numerator.astype(jnp.bfloat16)
        lanes = jnp.where(column_ids == 0, peak, total)
        stats_out[index] = lanes.T[:8]
        for copy in answer_copies(index):
            copy.start()

    def add_linear(head, prefix, finishing):
        cut = head_columns(head)
        near = jnp.where(side > 0, near_sums[head], 0.0)
        prefix = jnp.where(pair > 0, prefix.astype(jnp.float32), 0.0) + near
        coarse, fine = two_terms(feature(q_ref[:, cut].astype(jnp.float32)))
        sums, rest = two_terms(prefix)
        linear = sum(
            jnp.dot(left, right, preferred_element_type=jnp.float32)
            for left, right in ((coarse, sums), (fine, sums), (coarse, rest))
        )
        gain = scale_ref[head] / (width * math.sqrt(rows * blocks))
        linear = gain * linear
        if finishing:
            out_ref[:, cut] = (acc[:, cut] + linear).astype(out_ref.dtype)
        else:
            acc[:, cut] = linear

    def prepare(step):
        chunk = place(step, side)

        @pl.when((step < half) | (side > 0))
        def _():
            for offset in range(per_chunk):
                head = chunk * per_chunk + offset
                cut = head_columns(head)
                near_sums[head] = key_value_sum(far[0, 0, :, cut], far[0, 1, :, cut], lengths[1])

        @pl.when((step < half) & (pair < pairs - 1))
        def _():
            for offset in range(per_chunk):
                cut = head_columns(chunk * per_chunk + offset)
                own_sums[step * per_chunk + offset] = key_value_sum(k_ref[:, cut], v_ref[:, cut], lengths[0])

    def prepare_group(group):
        near_arrival(group).wait_recv()
        for offset in range(step_count):
            prepare(group * step_count + offset)

    def pass_on(number):
        @pl.when(pair > 0)
        def _():
            chain_copy(number).wait_recv()

        @pl.when(pair < pairs - 1)
        def _():
            for part in range(step_count):
                link = number * step_count + part
                first = place(link, side) * per_chunk
                for offset in range(per_chunk):
                    both = own_sums[link * per_chunk + offset] + near_sums[first + offset]
                    before = jnp.where(pair > 0, chain_in[link, offset].astype(jnp.float32), 0.0)
                    chain_out[link, offset] = (both + before).astype(jnp.bfloat16)
            chain_copy(number).start()

        @pl.when(pair > 0)
        def _():
            swap_copy(number).start()

    def linear_round(number):
        @pl.when(pair > 0)
        def _():
            swap_copy(number).wait_recv()

        for part in range(step_count):
            finish_linear(number * step_count + part)

    def finish_linear(late):
        for offset in range(per_chunk):
            add_linear(place(late, side) * per_chunk + offset, chain_in[late, offset], True)

        def other(finishing):
            for offset in range(per_chunk):
                add_linear(place(late, 1 - side) * per_chunk + offset, swap_in[late, offset], finishing)

        if joined:
            pl.when(late < half - 1)(lambda: other(True))
            pl.when(late == half - 1)(lambda: other(False))
        else:
            other(True)

    def one_turn(turn, _):
        pl.when(turn < chunks // step_count)(lambda: prepare_group(turn))
        number = turn - delay(pair)
        pl.when((number >= 0) & (number < rounds))(lambda: pass_on(number))
        lax.fori_loop(sent_by(turn - 1), sent_by(turn), lambda chunk, _: (send_far(chunk), 0)[1], 0)
        pl.when((turn >= linear_lag) & (turn - linear_lag < rounds))(lambda: linear_round(turn - linear_lag))

        if serve:
            @pl.when((pair < pairs // 2) & (turn > 0) & (turn <= serve))
            def _():
                answer(turn - 1)

        asking = served(turn) & (lax.rem(pair, 2) == 1)
        inside = turn < (chunks - 1 if joined else chunks)
        if serve:
            pl.when(inside & jnp.logical_not(asking))(lambda: attend(turn, False, False))
            pl.when(inside & asking)(lambda: attend(turn, False, True))
        else:
            pl.when(inside)(lambda: attend(turn, False, False))
        if joined:
            last = turn == chunks - 1
            if serve:
                pl.when(last & jnp.logical_not(asking))(lambda: attend(turn, True, False))
                pl.when(last & asking)(lambda: attend(turn, True, True))
            else:
                pl.when(last)(lambda: attend(turn, True, False))

        return 0

    @pl.when(pair == 0)
    def _():
        def clear(turn, _):
            chain_in[turn] = jnp.zeros_like(chain_in[turn])
            swap_in[turn] = jnp.zeros_like(swap_in[turn])
            return 0

        lax.fori_loop(0, half, clear, 0)

    lax.fori_loop(0, turns, one_turn, 0)

    for part, source in enumerate((k_hbm, v_hbm)):
        departure(source, send_sem.at[0, part]).wait_send()
        for bit in range(1, levels):
            if serve:
                pl.when(pair != bit - 1)(departure(source, send_sem.at[bit, part]).wait_send)
                some = source.at[:, :(heads - serve) * width]
                pl.when(pair == bit - 1)(departure(some, send_sem.at[bit, part]).wait_send)
            else:
                departure(source, send_sem.at[bit, part]).wait_send()

    pl.when(pair < pairs - 1)(departure(chain_out, chain_send.at[0]).wait_send)
    pl.when(pair > 0)(departure(chain_in, swap_send.at[0]).wait_send)

    if serve:
        @pl.when(lax.rem(pair, 2) == 1)
        def _():
            departure(guest_q, ask_send.at[0]).wait_send()

        @pl.when(pair < pairs // 2)
        def _():
            departure(served_out, answer_send.at[0]).wait_send()
            departure(stats_out, answer_send.at[1]).wait_send()


def delay(pair):
    return (LAG_TIMES * pair + 1) // LAG_OVER


def shards(blocks, query_rows, key_rows, value_rows, key_len, linear_scale):
    rows, total = query_rows.shape
    heads = linear_scale.shape[0]
    width = total // heads
    levels = blocks.bit_length() - 1
    chunks = heads // HEADS_PER_CHUNK
    half = chunks // 2
    step_count = STEPS if half % STEPS == 0 else 1
    serve = SERVED if blocks == 8 else 0
    guests = max(serve, 1)
    vmem = pl.BlockSpec(memory_space=pltpu.VMEM)
    hbm = pl.BlockSpec(memory_space=pltpu.HBM)
    piece = (half, HEADS_PER_CHUNK, width, width)
    dma = pltpu.SemaphoreType.DMA
    return pl.pallas_call(
        functools.partial(kernel, blocks, heads, width, HEADS_PER_CHUNK, WINDOW, CALM, delay, serve),
        out_shape=jax.ShapeDtypeStruct((rows, total), query_rows.dtype),
        in_specs=[hbm, hbm, hbm, hbm, hbm],
        out_specs=vmem,
        scratch_shapes=[
            pltpu.SMEM((blocks,), jnp.int32),
            pltpu.SMEM((heads,), jnp.float32),
            pltpu.VMEM((rows, total), jnp.bfloat16),
            pltpu.VMEM((rows, total), jnp.bfloat16),
            pltpu.VMEM((rows, total), jnp.bfloat16),
            dma((5,)),
            pltpu.VMEM((levels, 2, rows, total), jnp.bfloat16),
            pltpu.VMEM((rows, total), jnp.float32),
            pltpu.VMEM((heads // 2, width, width), jnp.float32),
            pltpu.VMEM((heads, width, width), jnp.float32),
            pltpu.VMEM(piece, jnp.bfloat16),
            pltpu.VMEM(piece, jnp.bfloat16),
            pltpu.VMEM(piece, jnp.bfloat16),
            dma((levels, 2)),
            dma((levels - 1, chunks + 1)),
            dma((chunks // step_count,)),
            dma((1,)),
            dma((half // step_count,)),
            dma((1,)),
            dma((half // step_count,)),
            pltpu.VMEM((guests, rows, width), jnp.bfloat16),
            pltpu.VMEM((guests, rows, width), jnp.bfloat16),
            pltpu.VMEM((guests, rows, width), jnp.bfloat16),
            pltpu.VMEM((guests, 8, rows), jnp.float32),
            pltpu.VMEM((guests, 8, rows), jnp.float32),
            dma((1,)),
            dma((1,)),
            dma((2,)),
            dma((guests, 2)),
        ],
        compiler_params=pltpu.CompilerParams(
            collective_id=0, has_side_effects=True, vmem_limit_bytes=55000000
        ),
        name="butterfly",
    )(
        pltpu.with_memory_space_constraint(key_len, pltpu.HBM),
        pltpu.with_memory_space_constraint(linear_scale, pltpu.HBM),
        query_rows, key_rows, value_rows,
    )


def solution(mesh):
    return jax.shard_map(
        functools.partial(shards, mesh.shape["seq"]),
        mesh=mesh,
        in_specs=(
            P(("groups", "seq"), "head"),
            P(("groups", "seq"), "head"),
            P(("groups", "seq"), "head"),
            P("groups"),
            P("head"),
        ),
        out_specs=P(("groups", "seq"), "head"),
        check_vma=False,
    )
```

```python
import functools
import math

import jax
import jax.numpy as jnp
from jax import lax
from jax.experimental import pallas as pl
from jax.experimental.pallas import tpu as pltpu
from jax.sharding import PartitionSpec as P

HEADS_PER_CHUNK = 2
WINDOW = 3
STEPS = 2
CALM = 3
SERVED = 5
LAG_TIMES = 6
LAG_OVER = 3


def feature(inputs):
    return jnp.where(inputs > 0.0, inputs + 1.0, jnp.exp(jnp.minimum(inputs, 0.0)))


def two_terms(wide):
    coarse = wide.astype(jnp.bfloat16)
    return coarse, (wide - coarse.astype(jnp.float32)).astype(jnp.bfloat16)


def kernel(
    blocks, heads, width, per_chunk, window, calm, delay, serve,
    len_hbm, scale_hbm, q_hbm, k_hbm, v_hbm, out_ref,
    len_ref, scale_ref, q_ref, k_ref, v_ref, load_sem, far, acc, own_sums, near_sums, chain_out, chain_in, swap_in,
    send_sem, recv_sem, near_recv, chain_send, chain_recv, swap_send, swap_recv,
    guest_q, served_out, served_in, stats_out, stats_in, ask_send, ask_recv, answer_send, answer_recv,
):
    rows = q_ref.shape[0]
    levels = blocks.bit_length() - 1
    chunks = heads // per_chunk
    half = chunks // 2
    pairs = blocks // 2
    span = per_chunk * width
    step_count = STEPS if half % STEPS == 0 else 1
    rounds = half // step_count
    linear_lag = max(chunks - rounds, delay(pairs - 1) + 1)
    joined = linear_lag + rounds == chunks
    turns = linear_lag + rounds

    me = lax.axis_index("seq")
    side = lax.rem(me, 2)
    pair = me // 2
    partners = [me + (1 - 2 * lax.rem(me // (1 << bit), 2)) * (1 << bit) for bit in range(levels)]
    above = lax.rem(me + 2, blocks)
    below = lax.rem(me + blocks - 2, blocks)

    def place(turn, which):
        return lax.rem(turn + half * which, chunks)

    def columns(chunk):
        return pl.ds(pl.multiple_of(chunk * span, span), span)

    def head_columns(head):
        return pl.ds(pl.multiple_of(head * width, width), width)

    def slot(turn, part):
        return jnp.where(turn == chunks - 1, chunks, turn) if joined and part else turn

    def arrival(place_in_far, received):
        return pltpu.make_async_remote_copy(
            src_ref=place_in_far,
            dst_ref=place_in_far,
            send_sem=send_sem.at[0, 0],
            recv_sem=received,
            device_id={"seq": partners[0]},
            device_id_type=pl.DeviceIdType.MESH,
        )

    def near_arrival(group):
        start = place(group * step_count, side) * span
        cut = pl.ds(pl.multiple_of(start, span), step_count * span)
        return arrival(far.at[0, :, :, cut], near_recv.at[group])

    def far_arrival(bit, turn, count):
        cut = pl.ds(pl.multiple_of(place(turn, side) * span, span), count * width)
        return arrival(far.at[bit, :, :, cut], recv_sem.at[bit - 1, turn])

    def departure(source, sent):
        return pltpu.make_async_remote_copy(
            src_ref=source,
            dst_ref=source,
            send_sem=sent,
            recv_sem=near_recv.at[0],
            device_id={"seq": partners[0]},
            device_id_type=pl.DeviceIdType.MESH,
        )

    def block_copy(bit, turn, part, which, heads_sent=per_chunk):
        source = k_hbm if part == 0 else v_hbm
        cut = pl.ds(pl.multiple_of(place(turn, which) * span, span), heads_sent * width)
        return pltpu.make_async_remote_copy(
            src_ref=source.at[:, cut],
            dst_ref=far.at[bit, part, :, cut],
            send_sem=send_sem.at[bit, part],
            recv_sem=near_recv.at[turn // step_count] if isinstance(bit, int) and bit == 0 else recv_sem.at[bit - 1, slot(turn, part)],
            device_id={"seq": partners[bit] if isinstance(bit, int) else partners[1]},
            device_id_type=pl.DeviceIdType.MESH,
        )

    def in_round(number):
        return pl.ds(number * step_count, step_count)

    def chain_copy(number):
        return pltpu.make_async_remote_copy(
            src_ref=chain_out.at[in_round(number)],
            dst_ref=chain_in.at[in_round(number)],
            send_sem=chain_send.at[0],
            recv_sem=chain_recv.at[number],
            device_id={"seq": above},
            device_id_type=pl.DeviceIdType.MESH,
        )

    def swap_copy(number):
        return pltpu.make_async_remote_copy(
            src_ref=chain_in.at[in_round(number)],
            dst_ref=swap_in.at[in_round(number)],
            send_sem=swap_send.at[0],
            recv_sem=swap_recv.at[number],
            device_id={"seq": partners[0]},
            device_id_type=pl.DeviceIdType.MESH,
        )

    host = jnp.where(pair == 1, below, partners[-1])
    guest = jnp.where(pair == 0, above, partners[-1])

    def served(turn):
        return (turn >= chunks - serve) & (turn < chunks) if serve else False

    def served_turn(index):
        return chunks - serve + index

    def served_index(turn):
        return turn - (chunks - serve)

    def withheld(bit, turn):
        return served(turn) & (pair == bit - 1)

    def ask_copy(index):
        return pltpu.make_async_remote_copy(
            src_ref=q_hbm.at[:, head_columns((place(served_turn(index), side) + 1) * per_chunk - 1)],
            dst_ref=guest_q.at[index],
            send_sem=ask_send.at[0],
            recv_sem=ask_recv.at[0],
            device_id={"seq": host},
            device_id_type=pl.DeviceIdType.MESH,
        )

    def answer_copies(index):
        return [
            pltpu.make_async_remote_copy(
                src_ref=source.at[index],
                dst_ref=target.at[index],
                send_sem=answer_send.at[part],
                recv_sem=answer_recv.at[index, part],
                device_id={"seq": guest},
                device_id_type=pl.DeviceIdType.MESH,
            )
            for part, (source, target) in enumerate(((served_out, served_in), (stats_out, stats_in)))
        ]

    loads = [
        pltpu.make_async_copy(source, target, load_sem.at[index])
        for index, (source, target) in enumerate(
            ((k_hbm, k_ref), (v_hbm, v_ref), (q_hbm, q_ref), (len_hbm, len_ref), (scale_hbm, scale_ref))
        )
    ]
    barrier = pltpu.get_barrier_semaphore()

    def greet(other):
        pl.semaphore_signal(
            barrier, inc=1, device_id={"seq": other}, device_id_type=pl.DeviceIdType.MESH
        )

    for other in partners:
        greet(other)
    pl.when(pair < pairs - 1)(lambda: greet(above))
    pl.when(pair > 0)(lambda: greet(below))
    for load in loads:
        load.start()
    pl.semaphore_wait(barrier, len(partners) + jnp.where((pair > 0) & (pair < pairs - 1), 2, 1))

    def for_each_far(turn, action):
        if serve:
            for part in range(2):
                for bit in range(1, levels):
                    less = withheld(bit, turn)
                    pl.when(jnp.logical_not(less))(lambda: action(block_copy(bit, turn, part, side)))
                    pl.when(less)(lambda: action(block_copy(bit, turn, part, side, per_chunk - 1)))
            return
        for part in range(2):
            for bit in range(1, levels):
                action(block_copy(bit, turn, part, side))

    def send_far(turn):
        for_each_far(turn, lambda copy: copy.start())

    def send_near(turn, _):
        for part in range(2):
            block_copy(0, turn, part, 1 - side).start()
        return 0

    def sent_by(turn):
        more = jnp.maximum(turn - delay(pair) - calm, 0)
        return jnp.minimum(window + turn + 1 + more, chunks)

    if serve:
        @pl.when(lax.rem(pair, 2) == 1)
        def _():
            for index in range(serve):
                ask_copy(index).start()

    lax.fori_loop(0, sent_by(-1), lambda turn, _: (send_far(turn), 0)[1], 0)
    lax.fori_loop(0, chunks, send_near, 0)

    row_ids = lax.broadcasted_iota(jnp.int32, (rows, rows), 0)
    column_ids = lax.broadcasted_iota(jnp.int32, (rows, rows), 1)
    live_rows = lax.broadcasted_iota(jnp.int32, (rows, width), 0)
    root = 1.0 / math.sqrt(width)

    for load in loads:
        load.wait()
    lengths = [len_ref[me]] + [len_ref[partner] for partner in partners]

    def key_value_sum(keys, values, length):
        mapped = jnp.where(live_rows < length, feature(keys.astype(jnp.float32)), 0.0)
        return sum(
            lax.dot_general(
                term, values, (((0,), (0,)), ((), ())), preferred_element_type=jnp.float32
            )
            for term in two_terms(mapped)
        )

    def piece(queries, keys, values, length, causal):
        weights, peak, total = weigh(queries, keys, length, causal)
        return jnp.dot(weights, values, preferred_element_type=jnp.float32), peak, total

    def weigh(queries, keys, length, causal):
        scores = root * lax.dot_general(
            queries, keys, (((1,), (1,)), ((), ())), preferred_element_type=jnp.float32
        )
        allowed = column_ids < length
        if causal:
            allowed = allowed & (column_ids <= row_ids)
        peak = jnp.max(jnp.where(allowed, scores, -jnp.inf), axis=1, keepdims=True)
        weights = jnp.where(allowed, jnp.exp(scores - peak), 0.0).astype(jnp.bfloat16)
        total = jnp.sum(weights.astype(jnp.float32), axis=1, keepdims=True)
        return weights, peak, total

    def merge(pieces):
        top = functools.reduce(jnp.maximum, [peak for _, peak, _ in pieces])
        numerator, denominator = 0.0, 0.0
        for part, peak, total in pieces:
            factor = jnp.exp(peak - top)
            numerator = numerator + factor * part
            denominator = denominator + factor * total
        return numerator / denominator

    def attend(turn, finishing, asked):
        chunk = place(turn, side)
        cuts = [head_columns(chunk * per_chunk + offset) for offset in range(per_chunk)]
        pieces = [
            [
                piece(q_ref[:, cut], k_ref[:, cut], v_ref[:, cut], lengths[0], True),
                piece(q_ref[:, cut], far[0, 0, :, cut], far[0, 1, :, cut], lengths[1], False),
            ]
            for cut in cuts
        ]
        if asked:
            full, cut_short = jnp.where(pair == 1, 2, 1), jnp.where(pair == 1, 1, 2)
            sources = [
                (full, jnp.where(pair == 1, lengths[3], lengths[2]), per_chunk),
                (cut_short, jnp.where(pair == 1, lengths[2], lengths[3]), per_chunk - 1),
            ]
            index = served_index(turn)
            for copy in answer_copies(index):
                copy.wait_recv()
            columns_of = jnp.tile(stats_in[index], (rows // 8, 1)).T
            pieces[-1].append((served_in[index].astype(jnp.float32), columns_of[:, :1], columns_of[:, 1:2]))
        else:
            sources = [(bit, lengths[1 + bit], per_chunk) for bit in range(1, levels)]
        if finishing:
            heavy = []
            for bit, extent, count in sources:
                block_copy(bit, turn, 0, side, count).wait_recv()
                heavy.append([weigh(q_ref[:, cut], far[bit, 0, :, cut], extent, False) for cut in cuts[:count]])
            for (bit, extent, count), weighed in zip(sources, heavy):
                block_copy(bit, turn, 1, side, count).wait_recv()
                for cut, found, (weights, peak, total) in zip(cuts, pieces, weighed):
                    numerator = jnp.dot(weights, far[bit, 1, :, cut], preferred_element_type=jnp.float32)
                    found.append((numerator, peak, total))
        else:
            for bit, extent, count in sources:
                far_arrival(bit, turn, count).wait_recv()
                for cut, found in list(zip(cuts, pieces))[:count]:
                    found.append(piece(q_ref[:, cut], far[bit, 0, :, cut], far[bit, 1, :, cut], extent, False))
        for cut, found in zip(cuts, pieces):
            attention = merge(found)
            if finishing:
                out_ref[:, cut] = (attention + acc[:, cut]).astype(out_ref.dtype)
            else:
                acc[:, cut] = attention

    def answer(index):
        @pl.when(index == 0)
        def _():
            arrival(guest_q, ask_recv.at[0]).wait_recv()

        cut = head_columns((place(served_turn(index), side) + 1) * per_chunk - 1)
        numerator, peak, total = piece(guest_q[index], k_ref[:, cut], v_ref[:, cut], lengths[0], False)
        served_out[index] = numerator.astype(jnp.bfloat16)
        lanes = jnp.where(column_ids == 0, peak, total)
        stats_out[index] = lanes.T[:8]
        for copy in answer_copies(index):
            copy.start()

    def add_linear(head, prefix, finishing):
        cut = head_columns(head)
        near = jnp.where(side > 0, near_sums[head], 0.0)
        prefix = jnp.where(pair > 0, prefix.astype(jnp.float32), 0.0) + near
        coarse, fine = two_terms(feature(q_ref[:, cut].astype(jnp.float32)))
        sums, rest = two_terms(prefix)
        linear = sum(
            jnp.dot(left, right, preferred_element_type=jnp.float32)
            for left, right in ((coarse, sums), (fine, sums), (coarse, rest))
        )
        gain = scale_ref[head] / (width * math.sqrt(rows * blocks))
        linear = gain * linear
        if finishing:
            out_ref[:, cut] = (acc[:, cut] + linear).astype(out_ref.dtype)
        else:
            acc[:, cut] = linear

    def prepare(step):
        chunk = place(step, side)

        @pl.when((step < half) | (side > 0))
        def _():
            for offset in range(per_chunk):
                head = chunk * per_chunk + offset
                cut = head_columns(head)
                near_sums[head] = key_value_sum(far[0, 0, :, cut], far[0, 1, :, cut], lengths[1])

        @pl.when((step < half) & (pair < pairs - 1))
        def _():
            for offset in range(per_chunk):
                cut = head_columns(chunk * per_chunk + offset)
                own_sums[step * per_chunk + offset] = key_value_sum(k_ref[:, cut], v_ref[:, cut], lengths[0])

    def prepare_group(group):
        near_arrival(group).wait_recv()
        for offset in range(step_count):
            prepare(group * step_count + offset)

    def pass_on(number):
        @pl.when(pair > 0)
        def _():
            chain_copy(number).wait_recv()

        @pl.when(pair < pairs - 1)
        def _():
            for part in range(step_count):
                link = number * step_count + part
                first = place(link, side) * per_chunk
                for offset in range(per_chunk):
                    both = own_sums[link * per_chunk + offset] + near_sums[first + offset]
                    before = jnp.where(pair > 0, chain_in[link, offset].astype(jnp.float32), 0.0)
                    chain_out[link, offset] = (both + before).astype(jnp.bfloat16)
            chain_copy(number).start()

        @pl.when(pair > 0)
        def _():
            swap_copy(number).start()

    def linear_round(number):
        @pl.when(pair > 0)
        def _():
            swap_copy(number).wait_recv()

        for part in range(step_count):
            finish_linear(number * step_count + part)

    def finish_linear(late):
        for offset in range(per_chunk):
            add_linear(place(late, side) * per_chunk + offset, chain_in[late, offset], True)

        def other(finishing):
            for offset in range(per_chunk):
                add_linear(place(late, 1 - side) * per_chunk + offset, swap_in[late, offset], finishing)

        if joined:
            pl.when(late < half - 1)(lambda: other(True))
            pl.when(late == half - 1)(lambda: other(False))
        else:
            other(True)

    def one_turn(turn, _):
        pl.when(turn < chunks // step_count)(lambda: prepare_group(turn))
        number = turn - delay(pair)
        pl.when((number >= 0) & (number < rounds))(lambda: pass_on(number))
        lax.fori_loop(sent_by(turn - 1), sent_by(turn), lambda chunk, _: (send_far(chunk), 0)[1], 0)
        pl.when((turn >= linear_lag) & (turn - linear_lag < rounds))(lambda: linear_round(turn - linear_lag))

        if serve:
            @pl.when((pair < pairs // 2) & (turn > 0) & (turn <= serve))
            def _():
                answer(turn - 1)

        asking = served(turn) & (lax.rem(pair, 2) == 1)
        inside = turn < (chunks - 1 if joined else chunks)
        if serve:
            pl.when(inside & jnp.logical_not(asking))(lambda: attend(turn, False, False))
            pl.when(inside & asking)(lambda: attend(turn, False, True))
        else:
            pl.when(inside)(lambda: attend(turn, False, False))
        if joined:
            last = turn == chunks - 1
            if serve:
                pl.when(last & jnp.logical_not(asking))(lambda: attend(turn, True, False))
                pl.when(last & asking)(lambda: attend(turn, True, True))
            else:
                pl.when(last)(lambda: attend(turn, True, False))

        return 0

    @pl.when(pair == 0)
    def _():
        def clear(turn, _):
            chain_in[turn] = jnp.zeros_like(chain_in[turn])
            swap_in[turn] = jnp.zeros_like(swap_in[turn])
            return 0

        lax.fori_loop(0, half, clear, 0)

    lax.fori_loop(0, turns, one_turn, 0)

    for part, source in enumerate((k_hbm, v_hbm)):
        departure(source, send_sem.at[0, part]).wait_send()
        for bit in range(1, levels):
            if serve:
                pl.when(pair != bit - 1)(departure(source, send_sem.at[bit, part]).wait_send)
                some = source.at[:, :(heads - serve) * width]
                pl.when(pair == bit - 1)(departure(some, send_sem.at[bit, part]).wait_send)
            else:
                departure(source, send_sem.at[bit, part]).wait_send()

    pl.when(pair < pairs - 1)(departure(chain_out, chain_send.at[0]).wait_send)
    pl.when(pair > 0)(departure(chain_in, swap_send.at[0]).wait_send)

    if serve:
        @pl.when(lax.rem(pair, 2) == 1)
        def _():
            departure(guest_q, ask_send.at[0]).wait_send()

        @pl.when(pair < pairs // 2)
        def _():
            departure(served_out, answer_send.at[0]).wait_send()
            departure(stats_out, answer_send.at[1]).wait_send()


def delay(pair):
    return (LAG_TIMES * pair + 1) // LAG_OVER


def shards(blocks, query_rows, key_rows, value_rows, key_len, linear_scale):
    rows, total = query_rows.shape
    heads = linear_scale.shape[0]
    width = total // heads
    levels = blocks.bit_length() - 1
    chunks = heads // HEADS_PER_CHUNK
    half = chunks // 2
    step_count = STEPS if half % STEPS == 0 else 1
    serve = SERVED if blocks == 8 else 0
    guests = max(serve, 1)
    vmem = pl.BlockSpec(memory_space=pltpu.VMEM)
    hbm = pl.BlockSpec(memory_space=pltpu.HBM)
    piece = (half, HEADS_PER_CHUNK, width, width)
    dma = pltpu.SemaphoreType.DMA
    return pl.pallas_call(
        functools.partial(kernel, blocks, heads, width, HEADS_PER_CHUNK, WINDOW, CALM, delay, serve),
        out_shape=jax.ShapeDtypeStruct((rows, total), query_rows.dtype),
        in_specs=[hbm, hbm, hbm, hbm, hbm],
        out_specs=vmem,
        scratch_shapes=[
            pltpu.SMEM((blocks,), jnp.int32),
            pltpu.SMEM((heads,), jnp.float32),
            pltpu.VMEM((rows, total), jnp.bfloat16),
            pltpu.VMEM((rows, total), jnp.bfloat16),
            pltpu.VMEM((rows, total), jnp.bfloat16),
            dma((5,)),
            pltpu.VMEM((levels, 2, rows, total), jnp.bfloat16),
            pltpu.VMEM((rows, total), jnp.float32),
            pltpu.VMEM((heads // 2, width, width), jnp.float32),
            pltpu.VMEM((heads, width, width), jnp.float32),
            pltpu.VMEM(piece, jnp.bfloat16),
            pltpu.VMEM(piece, jnp.bfloat16),
            pltpu.VMEM(piece, jnp.bfloat16),
            dma((levels, 2)),
            dma((levels - 1, chunks + 1)),
            dma((chunks // step_count,)),
            dma((1,)),
            dma((half // step_count,)),
            dma((1,)),
            dma((half // step_count,)),
            pltpu.VMEM((guests, rows, width), jnp.bfloat16),
            pltpu.VMEM((guests, rows, width), jnp.bfloat16),
            pltpu.VMEM((guests, rows, width), jnp.bfloat16),
            pltpu.VMEM((guests, 8, rows), jnp.float32),
            pltpu.VMEM((guests, 8, rows), jnp.float32),
            dma((1,)),
            dma((1,)),
            dma((2,)),
            dma((guests, 2)),
        ],
        compiler_params=pltpu.CompilerParams(
            collective_id=0, has_side_effects=True, vmem_limit_bytes=55000000
        ),
        name="butterfly",
    )(
        pltpu.with_memory_space_constraint(key_len, pltpu.HBM),
        pltpu.with_memory_space_constraint(linear_scale, pltpu.HBM),
        query_rows, key_rows, value_rows,
    )


def solution(mesh):
    return jax.shard_map(
        functools.partial(shards, mesh.shape["seq"]),
        mesh=mesh,
        in_specs=(
            P(("groups", "seq"), "head"),
            P(("groups", "seq"), "head"),
            P(("groups", "seq"), "head"),
            P("groups"),
            P("head"),
        ),
        out_specs=P(("groups", "seq"), "head"),
        check_vma=False,
    )
```

```python
import functools
import math

import jax
import jax.numpy as jnp
from jax import lax
from jax.experimental import pallas as pl
from jax.experimental.pallas import tpu as pltpu
from jax.sharding import PartitionSpec as P

HEADS_PER_CHUNK = 2
WINDOW = 3
STEPS = 2
CALM = 3
SERVED = 5
LAG_TIMES = 6
LAG_OVER = 3


def feature(inputs):
    return jnp.where(inputs > 0.0, inputs + 1.0, jnp.exp(jnp.minimum(inputs, 0.0)))


def two_terms(wide):
    coarse = wide.astype(jnp.bfloat16)
    return coarse, (wide - coarse.astype(jnp.float32)).astype(jnp.bfloat16)


def kernel(
    blocks, heads, width, per_chunk, window, calm, delay, serve,
    len_hbm, scale_hbm, q_hbm, k_hbm, v_hbm, out_ref,
    len_ref, scale_ref, q_ref, k_ref, v_ref, load_sem, far, acc, own_sums, near_sums, chain_out, chain_in, swap_in,
    send_sem, recv_sem, near_recv, chain_send, chain_recv, swap_send, swap_recv,
    guest_q, served_out, served_in, stats_out, stats_in, ask_send, ask_recv, answer_send, answer_recv,
):
    rows = q_ref.shape[0]
    levels = blocks.bit_length() - 1
    chunks = heads // per_chunk
    half = chunks // 2
    pairs = blocks // 2
    span = per_chunk * width
    step_count = STEPS if half % STEPS == 0 else 1
    rounds = half // step_count
    linear_lag = max(chunks - rounds, delay(pairs - 1) + 1)
    joined = linear_lag + rounds == chunks
    turns = linear_lag + rounds

    me = lax.axis_index("seq")
    side = lax.rem(me, 2)
    pair = me // 2
    partners = [me + (1 - 2 * lax.rem(me // (1 << bit), 2)) * (1 << bit) for bit in range(levels)]
    above = lax.rem(me + 2, blocks)
    below = lax.rem(me + blocks - 2, blocks)

    def place(turn, which):
        return lax.rem(turn + half * which, chunks)

    def columns(chunk):
        return pl.ds(pl.multiple_of(chunk * span, span), span)

    def head_columns(head):
        return pl.ds(pl.multiple_of(head * width, width), width)

    def slot(turn, part):
        return jnp.where(turn == chunks - 1, chunks, turn) if joined and part else turn

    def arrival(place_in_far, received):
        return pltpu.make_async_remote_copy(
            src_ref=place_in_far,
            dst_ref=place_in_far,
            send_sem=send_sem.at[0, 0],
            recv_sem=received,
            device_id={"seq": partners[0]},
            device_id_type=pl.DeviceIdType.MESH,
        )

    def near_arrival(group):
        start = place(group * step_count, side) * span
        cut = pl.ds(pl.multiple_of(start, span), step_count * span)
        return arrival(far.at[0, :, :, cut], near_recv.at[group])

    def far_arrival(bit, turn, count):
        cut = pl.ds(pl.multiple_of(place(turn, side) * span, span), count * width)
        return arrival(far.at[bit, :, :, cut], recv_sem.at[bit - 1, turn])

    def departure(source, sent):
        return pltpu.make_async_remote_copy(
            src_ref=source,
            dst_ref=source,
            send_sem=sent,
            recv_sem=near_recv.at[0],
            device_id={"seq": partners[0]},
            device_id_type=pl.DeviceIdType.MESH,
        )

    def block_copy(bit, turn, part, which, heads_sent=per_chunk):
        source = k_hbm if part == 0 else v_hbm
        cut = pl.ds(pl.multiple_of(place(turn, which) * span, span), heads_sent * width)
        return pltpu.make_async_remote_copy(
            src_ref=source.at[:, cut],
            dst_ref=far.at[bit, part, :, cut],
            send_sem=send_sem.at[bit, part],
            recv_sem=near_recv.at[turn // step_count] if isinstance(bit, int) and bit == 0 else recv_sem.at[bit - 1, slot(turn, part)],
            device_id={"seq": partners[bit] if isinstance(bit, int) else partners[1]},
            device_id_type=pl.DeviceIdType.MESH,
        )

    def in_round(number):
        return pl.ds(number * step_count, step_count)

    def chain_copy(number):
        return pltpu.make_async_remote_copy(
            src_ref=chain_out.at[in_round(number)],
            dst_ref=chain_in.at[in_round(number)],
            send_sem=chain_send.at[0],
            recv_sem=chain_recv.at[number],
            device_id={"seq": above},
            device_id_type=pl.DeviceIdType.MESH,
        )

    def swap_copy(number):
        return pltpu.make_async_remote_copy(
            src_ref=chain_in.at[in_round(number)],
            dst_ref=swap_in.at[in_round(number)],
            send_sem=swap_send.at[0],
            recv_sem=swap_recv.at[number],
            device_id={"seq": partners[0]},
            device_id_type=pl.DeviceIdType.MESH,
        )

    host = jnp.where(pair == 1, below, partners[-1])
    guest = jnp.where(pair == 0, above, partners[-1])

    def served(turn):
        return (turn >= chunks - serve) & (turn < chunks) if serve else False

    def served_turn(index):
        return chunks - serve + index

    def served_index(turn):
        return turn - (chunks - serve)

    def withheld(bit, turn):
        return served(turn) & (pair == bit - 1)

    def ask_copy(index):
        return pltpu.make_async_remote_copy(
            src_ref=q_hbm.at[:, head_columns((place(served_turn(index), side) + 1) * per_chunk - 1)],
            dst_ref=guest_q.at[index],
            send_sem=ask_send.at[0],
            recv_sem=ask_recv.at[0],
            device_id={"seq": host},
            device_id_type=pl.DeviceIdType.MESH,
        )

    def answer_copies(index):
        return [
            pltpu.make_async_remote_copy(
                src_ref=source.at[index],
                dst_ref=target.at[index],
                send_sem=answer_send.at[part],
                recv_sem=answer_recv.at[index, part],
                device_id={"seq": guest},
                device_id_type=pl.DeviceIdType.MESH,
            )
            for part, (source, target) in enumerate(((served_out, served_in), (stats_out, stats_in)))
        ]

    loads = [
        pltpu.make_async_copy(source, target, load_sem.at[index])
        for index, (source, target) in enumerate(
            ((k_hbm, k_ref), (v_hbm, v_ref), (q_hbm, q_ref), (len_hbm, len_ref), (scale_hbm, scale_ref))
        )
    ]
    barrier = pltpu.get_barrier_semaphore()

    def greet(other):
        pl.semaphore_signal(
            barrier, inc=1, device_id={"seq": other}, device_id_type=pl.DeviceIdType.MESH
        )

    for other in partners:
        greet(other)
    pl.when(pair < pairs - 1)(lambda: greet(above))
    pl.when(pair > 0)(lambda: greet(below))
    for load in loads:
        load.start()
    pl.semaphore_wait(barrier, len(partners) + jnp.where((pair > 0) & (pair < pairs - 1), 2, 1))

    def for_each_far(turn, action):
        if serve:
            for part in range(2):
                for bit in reversed(range(1, levels)):
                    less = withheld(bit, turn)
                    pl.when(jnp.logical_not(less))(lambda: action(block_copy(bit, turn, part, side)))
                    pl.when(less)(lambda: action(block_copy(bit, turn, part, side, per_chunk - 1)))
            return
        for part in range(2):
            for bit in range(1, levels):
                action(block_copy(bit, turn, part, side))

    def send_far(turn):
        for_each_far(turn, lambda copy: copy.start())

    def send_near(turn, _):
        for part in range(2):
            block_copy(0, turn, part, 1 - side).start()
        return 0

    def sent_by(turn):
        more = jnp.maximum(turn - delay(pair) - calm, 0)
        return jnp.minimum(window + turn + 1 + more, chunks)

    if serve:
        @pl.when(lax.rem(pair, 2) == 1)
        def _():
            for index in range(serve):
                ask_copy(index).start()

    lax.fori_loop(0, sent_by(-1), lambda turn, _: (send_far(turn), 0)[1], 0)
    lax.fori_loop(0, chunks, send_near, 0)

    row_ids = lax.broadcasted_iota(jnp.int32, (rows, rows), 0)
    column_ids = lax.broadcasted_iota(jnp.int32, (rows, rows), 1)
    live_rows = lax.broadcasted_iota(jnp.int32, (rows, width), 0)
    root = 1.0 / math.sqrt(width)

    for load in loads:
        load.wait()
    lengths = [len_ref[me]] + [len_ref[partner] for partner in partners]

    def key_value_sum(keys, values, length):
        mapped = jnp.where(live_rows < length, feature(keys.astype(jnp.float32)), 0.0)
        return sum(
            lax.dot_general(
                term, values, (((0,), (0,)), ((), ())), preferred_element_type=jnp.float32
            )
            for term in two_terms(mapped)
        )

    def piece(queries, keys, values, length, causal):
        weights, peak, total = weigh(queries, keys, length, causal)
        return jnp.dot(weights, values, preferred_element_type=jnp.float32), peak, total

    def weigh(queries, keys, length, causal):
        scores = root * lax.dot_general(
            queries, keys, (((1,), (1,)), ((), ())), preferred_element_type=jnp.float32
        )
        allowed = column_ids < length
        if causal:
            allowed = allowed & (column_ids <= row_ids)
        peak = jnp.max(jnp.where(allowed, scores, -jnp.inf), axis=1, keepdims=True)
        weights = jnp.where(allowed, jnp.exp(scores - peak), 0.0).astype(jnp.bfloat16)
        total = jnp.sum(weights.astype(jnp.float32), axis=1, keepdims=True)
        return weights, peak, total

    def merge(pieces):
        top = functools.reduce(jnp.maximum, [peak for _, peak, _ in pieces])
        numerator, denominator = 0.0, 0.0
        for part, peak, total in pieces:
            factor = jnp.exp(peak - top)
            numerator = numerator + factor * part
            denominator = denominator + factor * total
        return numerator / denominator

    def attend(turn, finishing, asked):
        chunk = place(turn, side)
        cuts = [head_columns(chunk * per_chunk + offset) for offset in range(per_chunk)]
        pieces = [
            [
                piece(q_ref[:, cut], k_ref[:, cut], v_ref[:, cut], lengths[0], True),
                piece(q_ref[:, cut], far[0, 0, :, cut], far[0, 1, :, cut], lengths[1], False),
            ]
            for cut in cuts
        ]
        if asked:
            full, cut_short = jnp.where(pair == 1, 2, 1), jnp.where(pair == 1, 1, 2)
            sources = [
                (full, jnp.where(pair == 1, lengths[3], lengths[2]), per_chunk),
                (cut_short, jnp.where(pair == 1, lengths[2], lengths[3]), per_chunk - 1),
            ]
            index = served_index(turn)
            for copy in answer_copies(index):
                copy.wait_recv()
            columns_of = jnp.tile(stats_in[index], (rows // 8, 1)).T
            pieces[-1].append((served_in[index].astype(jnp.float32), columns_of[:, :1], columns_of[:, 1:2]))
        else:
            sources = [(bit, lengths[1 + bit], per_chunk) for bit in range(1, levels)]
        if finishing:
            heavy = []
            for bit, extent, count in sources:
                block_copy(bit, turn, 0, side, count).wait_recv()
                heavy.append([weigh(q_ref[:, cut], far[bit, 0, :, cut], extent, False) for cut in cuts[:count]])
            for (bit, extent, count), weighed in zip(sources, heavy):
                block_copy(bit, turn, 1, side, count).wait_recv()
                for cut, found, (weights, peak, total) in zip(cuts, pieces, weighed):
                    numerator = jnp.dot(weights, far[bit, 1, :, cut], preferred_element_type=jnp.float32)
                    found.append((numerator, peak, total))
        else:
            for bit, extent, count in sources:
                far_arrival(bit, turn, count).wait_recv()
                for cut, found in list(zip(cuts, pieces))[:count]:
                    found.append(piece(q_ref[:, cut], far[bit, 0, :, cut], far[bit, 1, :, cut], extent, False))
        for cut, found in zip(cuts, pieces):
            attention = merge(found)
            if finishing:
                out_ref[:, cut] = (attention + acc[:, cut]).astype(out_ref.dtype)
            else:
                acc[:, cut] = attention

    def answer(index):
        @pl.when(index == 0)
        def _():
            arrival(guest_q, ask_recv.at[0]).wait_recv()

        cut = head_columns((place(served_turn(index), side) + 1) * per_chunk - 1)
        numerator, peak, total = piece(guest_q[index], k_ref[:, cut], v_ref[:, cut], lengths[0], False)
        served_out[index] = numerator.astype(jnp.bfloat16)
        lanes = jnp.where(column_ids == 0, peak, total)
        stats_out[index] = lanes.T[:8]
        for copy in answer_copies(index):
            copy.start()

    def add_linear(head, prefix, finishing):
        cut = head_columns(head)
        near = jnp.where(side > 0, near_sums[head], 0.0)
        prefix = jnp.where(pair > 0, prefix.astype(jnp.float32), 0.0) + near
        coarse, fine = two_terms(feature(q_ref[:, cut].astype(jnp.float32)))
        sums, rest = two_terms(prefix)
        linear = sum(
            jnp.dot(left, right, preferred_element_type=jnp.float32)
            for left, right in ((coarse, sums), (fine, sums), (coarse, rest))
        )
        gain = scale_ref[head] / (width * math.sqrt(rows * blocks))
        linear = gain * linear
        if finishing:
            out_ref[:, cut] = (acc[:, cut] + linear).astype(out_ref.dtype)
        else:
            acc[:, cut] = linear

    def prepare(step):
        chunk = place(step, side)

        @pl.when((step < half) | (side > 0))
        def _():
            for offset in range(per_chunk):
                head = chunk * per_chunk + offset
                cut = head_columns(head)
                near_sums[head] = key_value_sum(far[0, 0, :, cut], far[0, 1, :, cut], lengths[1])

        @pl.when((step < half) & (pair < pairs - 1))
        def _():
            for offset in range(per_chunk):
                cut = head_columns(chunk * per_chunk + offset)
                own_sums[step * per_chunk + offset] = key_value_sum(k_ref[:, cut], v_ref[:, cut], lengths[0])

    def prepare_group(group):
        near_arrival(group).wait_recv()
        for offset in range(step_count):
            prepare(group * step_count + offset)

    def pass_on(number):
        @pl.when(pair > 0)
        def _():
            chain_copy(number).wait_recv()

        @pl.when(pair < pairs - 1)
        def _():
            for part in range(step_count):
                link = number * step_count + part
                first = place(link, side) * per_chunk
                for offset in range(per_chunk):
                    both = own_sums[link * per_chunk + offset] + near_sums[first + offset]
                    before = jnp.where(pair > 0, chain_in[link, offset].astype(jnp.float32), 0.0)
                    chain_out[link, offset] = (both + before).astype(jnp.bfloat16)
            chain_copy(number).start()

        @pl.when(pair > 0)
        def _():
            swap_copy(number).start()

    def linear_round(number):
        @pl.when(pair > 0)
        def _():
            swap_copy(number).wait_recv()

        for part in range(step_count):
            finish_linear(number * step_count + part)

    def finish_linear(late):
        for offset in range(per_chunk):
            add_linear(place(late, side) * per_chunk + offset, chain_in[late, offset], True)

        def other(finishing):
            for offset in range(per_chunk):
                add_linear(place(late, 1 - side) * per_chunk + offset, swap_in[late, offset], finishing)

        if joined:
            pl.when(late < half - 1)(lambda: other(True))
            pl.when(late == half - 1)(lambda: other(False))
        else:
            other(True)

    def one_turn(turn, _):
        pl.when(turn < chunks // step_count)(lambda: prepare_group(turn))
        number = turn - delay(pair)
        pl.when((number >= 0) & (number < rounds))(lambda: pass_on(number))
        lax.fori_loop(sent_by(turn - 1), sent_by(turn), lambda chunk, _: (send_far(chunk), 0)[1], 0)
        pl.when((turn >= linear_lag) & (turn - linear_lag < rounds))(lambda: linear_round(turn - linear_lag))

        if serve:
            @pl.when((pair < pairs // 2) & (turn > 0) & (turn <= serve))
            def _():
                answer(turn - 1)

        asking = served(turn) & (lax.rem(pair, 2) == 1)
        inside = turn < (chunks - 1 if joined else chunks)
        if serve:
            pl.when(inside & jnp.logical_not(asking))(lambda: attend(turn, False, False))
            pl.when(inside & asking)(lambda: attend(turn, False, True))
        else:
            pl.when(inside)(lambda: attend(turn, False, False))
        if joined:
            last = turn == chunks - 1
            if serve:
                pl.when(last & jnp.logical_not(asking))(lambda: attend(turn, True, False))
                pl.when(last & asking)(lambda: attend(turn, True, True))
            else:
                pl.when(last)(lambda: attend(turn, True, False))

        return 0

    @pl.when(pair == 0)
    def _():
        def clear(turn, _):
            chain_in[turn] = jnp.zeros_like(chain_in[turn])
            swap_in[turn] = jnp.zeros_like(swap_in[turn])
            return 0

        lax.fori_loop(0, half, clear, 0)

    lax.fori_loop(0, turns, one_turn, 0)

    for part, source in enumerate((k_hbm, v_hbm)):
        departure(source, send_sem.at[0, part]).wait_send()
        for bit in range(1, levels):
            if serve:
                pl.when(pair != bit - 1)(departure(source, send_sem.at[bit, part]).wait_send)
                some = source.at[:, :(heads - serve) * width]
                pl.when(pair == bit - 1)(departure(some, send_sem.at[bit, part]).wait_send)
            else:
                departure(source, send_sem.at[bit, part]).wait_send()

    pl.when(pair < pairs - 1)(departure(chain_out, chain_send.at[0]).wait_send)
    pl.when(pair > 0)(departure(chain_in, swap_send.at[0]).wait_send)

    if serve:
        @pl.when(lax.rem(pair, 2) == 1)
        def _():
            departure(guest_q, ask_send.at[0]).wait_send()

        @pl.when(pair < pairs // 2)
        def _():
            departure(served_out, answer_send.at[0]).wait_send()
            departure(stats_out, answer_send.at[1]).wait_send()


def delay(pair):
    return (LAG_TIMES * pair + 1) // LAG_OVER


def shards(blocks, query_rows, key_rows, value_rows, key_len, linear_scale):
    rows, total = query_rows.shape
    heads = linear_scale.shape[0]
    width = total // heads
    levels = blocks.bit_length() - 1
    chunks = heads // HEADS_PER_CHUNK
    half = chunks // 2
    step_count = STEPS if half % STEPS == 0 else 1
    serve = SERVED if blocks == 8 else 0
    guests = max(serve, 1)
    vmem = pl.BlockSpec(memory_space=pltpu.VMEM)
    hbm = pl.BlockSpec(memory_space=pltpu.HBM)
    piece = (half, HEADS_PER_CHUNK, width, width)
    dma = pltpu.SemaphoreType.DMA
    return pl.pallas_call(
        functools.partial(kernel, blocks, heads, width, HEADS_PER_CHUNK, WINDOW, CALM, delay, serve),
        out_shape=jax.ShapeDtypeStruct((rows, total), query_rows.dtype),
        in_specs=[hbm, hbm, hbm, hbm, hbm],
        out_specs=vmem,
        scratch_shapes=[
            pltpu.SMEM((blocks,), jnp.int32),
            pltpu.SMEM((heads,), jnp.float32),
            pltpu.VMEM((rows, total), jnp.bfloat16),
            pltpu.VMEM((rows, total), jnp.bfloat16),
            pltpu.VMEM((rows, total), jnp.bfloat16),
            dma((5,)),
            pltpu.VMEM((levels, 2, rows, total), jnp.bfloat16),
            pltpu.VMEM((rows, total), jnp.float32),
            pltpu.VMEM((heads // 2, width, width), jnp.float32),
            pltpu.VMEM((heads, width, width), jnp.float32),
            pltpu.VMEM(piece, jnp.bfloat16),
            pltpu.VMEM(piece, jnp.bfloat16),
            pltpu.VMEM(piece, jnp.bfloat16),
            dma((levels, 2)),
            dma((levels - 1, chunks + 1)),
            dma((chunks // step_count,)),
            dma((1,)),
            dma((half // step_count,)),
            dma((1,)),
            dma((half // step_count,)),
            pltpu.VMEM((guests, rows, width), jnp.bfloat16),
            pltpu.VMEM((guests, rows, width), jnp.bfloat16),
            pltpu.VMEM((guests, rows, width), jnp.bfloat16),
            pltpu.VMEM((guests, 8, rows), jnp.float32),
            pltpu.VMEM((guests, 8, rows), jnp.float32),
            dma((1,)),
            dma((1,)),
            dma((2,)),
            dma((guests, 2)),
        ],
        compiler_params=pltpu.CompilerParams(
            collective_id=0, has_side_effects=True, vmem_limit_bytes=55000000
        ),
        name="butterfly",
    )(
        pltpu.with_memory_space_constraint(key_len, pltpu.HBM),
        pltpu.with_memory_space_constraint(linear_scale, pltpu.HBM),
        query_rows, key_rows, value_rows,
    )


def solution(mesh):
    return jax.shard_map(
        functools.partial(shards, mesh.shape["seq"]),
        mesh=mesh,
        in_specs=(
            P(("groups", "seq"), "head"),
            P(("groups", "seq"), "head"),
            P(("groups", "seq"), "head"),
            P("groups"),
            P("head"),
        ),
        out_specs=P(("groups", "seq"), "head"),
        check_vma=False,
    )
```

```python
import functools
import math

import jax
import jax.numpy as jnp
from jax import lax
from jax.experimental import pallas as pl
from jax.experimental.pallas import tpu as pltpu
from jax.sharding import PartitionSpec as P

HEADS_PER_CHUNK = 2
WINDOW = 3
STEPS = 2
CALM = 3
SERVED = 5
LAG_TIMES = 6
LAG_OVER = 3


def feature(inputs):
    return jnp.where(inputs > 0.0, inputs + 1.0, jnp.exp(jnp.minimum(inputs, 0.0)))


def two_terms(wide):
    coarse = wide.astype(jnp.bfloat16)
    return coarse, (wide - coarse.astype(jnp.float32)).astype(jnp.bfloat16)


def kernel(
    blocks, heads, width, per_chunk, window, calm, delay, serve,
    len_hbm, scale_hbm, q_hbm, k_hbm, v_hbm, out_ref,
    len_ref, scale_ref, q_ref, k_ref, v_ref, load_sem, far, acc, own_sums, near_sums, chain_out, chain_in, swap_in,
    send_sem, recv_sem, near_recv, chain_send, chain_recv, swap_send, swap_recv,
    guest_q, served_out, served_in, stats_out, stats_in, ask_send, ask_recv, answer_send, answer_recv,
):
    rows = q_ref.shape[0]
    levels = blocks.bit_length() - 1
    chunks = heads // per_chunk
    half = chunks // 2
    pairs = blocks // 2
    span = per_chunk * width
    step_count = STEPS if half % STEPS == 0 else 1
    rounds = half // step_count
    linear_lag = max(chunks - rounds, delay(pairs - 1) + 1)
    joined = linear_lag + rounds == chunks
    turns = linear_lag + rounds

    me = lax.axis_index("seq")
    side = lax.rem(me, 2)
    pair = me // 2
    partners = [me + (1 - 2 * lax.rem(me // (1 << bit), 2)) * (1 << bit) for bit in range(levels)]
    above = lax.rem(me + 2, blocks)
    below = lax.rem(me + blocks - 2, blocks)

    def place(turn, which):
        return lax.rem(turn + half * which, chunks)

    def columns(chunk):
        return pl.ds(pl.multiple_of(chunk * span, span), span)

    def head_columns(head):
        return pl.ds(pl.multiple_of(head * width, width), width)

    def slot(turn, part):
        return jnp.where(turn == chunks - 1, chunks, turn) if joined and part else turn

    def arrival(place_in_far, received):
        return pltpu.make_async_remote_copy(
            src_ref=place_in_far,
            dst_ref=place_in_far,
            send_sem=send_sem.at[0, 0],
            recv_sem=received,
            device_id={"seq": partners[0]},
            device_id_type=pl.DeviceIdType.MESH,
        )

    def near_arrival(group):
        start = place(group * step_count, side) * span
        cut = pl.ds(pl.multiple_of(start, span), step_count * span)
        return arrival(far.at[0, :, :, cut], near_recv.at[group])

    def far_arrival(bit, turn, count):
        cut = pl.ds(pl.multiple_of(place(turn, side) * span, span), count * width)
        return arrival(far.at[bit, :, :, cut], recv_sem.at[bit - 1, turn])

    def departure(source, sent):
        return pltpu.make_async_remote_copy(
            src_ref=source,
            dst_ref=source,
            send_sem=sent,
            recv_sem=near_recv.at[0],
            device_id={"seq": partners[0]},
            device_id_type=pl.DeviceIdType.MESH,
        )

    def block_copy(bit, turn, part, which, heads_sent=per_chunk):
        source = k_hbm if part == 0 else v_hbm
        cut = pl.ds(pl.multiple_of(place(turn, which) * span, span), heads_sent * width)
        return pltpu.make_async_remote_copy(
            src_ref=source.at[:, cut],
            dst_ref=far.at[bit, part, :, cut],
            send_sem=send_sem.at[bit, part],
            recv_sem=near_recv.at[turn // step_count] if isinstance(bit, int) and bit == 0 else recv_sem.at[bit - 1, slot(turn, part)],
            device_id={"seq": partners[bit] if isinstance(bit, int) else partners[1]},
            device_id_type=pl.DeviceIdType.MESH,
        )

    def in_round(number):
        return pl.ds(number * step_count, step_count)

    def chain_copy(number):
        return pltpu.make_async_remote_copy(
            src_ref=chain_out.at[in_round(number)],
            dst_ref=chain_in.at[in_round(number)],
            send_sem=chain_send.at[0],
            recv_sem=chain_recv.at[number],
            device_id={"seq": above},
            device_id_type=pl.DeviceIdType.MESH,
        )

    def swap_copy(number):
        return pltpu.make_async_remote_copy(
            src_ref=chain_in.at[in_round(number)],
            dst_ref=swap_in.at[in_round(number)],
            send_sem=swap_send.at[0],
            recv_sem=swap_recv.at[number],
            device_id={"seq": partners[0]},
            device_id_type=pl.DeviceIdType.MESH,
        )

    host = jnp.where(pair == 1, below, partners[-1])
    guest = jnp.where(pair == 0, above, partners[-1])

    def served(turn):
        return (turn >= chunks - serve) & (turn < chunks) if serve else False

    def served_turn(index):
        return chunks - serve + index

    def served_index(turn):
        return turn - (chunks - serve)

    def withheld(bit, turn):
        return served(turn) & (pair == bit - 1)

    def ask_copy(index):
        return pltpu.make_async_remote_copy(
            src_ref=q_hbm.at[:, head_columns((place(served_turn(index), side) + 1) * per_chunk - 1)],
            dst_ref=guest_q.at[index],
            send_sem=ask_send.at[0],
            recv_sem=ask_recv.at[0],
            device_id={"seq": host},
            device_id_type=pl.DeviceIdType.MESH,
        )

    def answer_copies(index):
        return [
            pltpu.make_async_remote_copy(
                src_ref=source.at[index],
                dst_ref=target.at[index],
                send_sem=answer_send.at[part],
                recv_sem=answer_recv.at[index, part],
                device_id={"seq": guest},
                device_id_type=pl.DeviceIdType.MESH,
            )
            for part, (source, target) in enumerate(((served_out, served_in), (stats_out, stats_in)))
        ]

    loads = [
        pltpu.make_async_copy(source, target, load_sem.at[index])
        for index, (source, target) in enumerate(
            ((k_hbm, k_ref), (v_hbm, v_ref), (q_hbm, q_ref), (len_hbm, len_ref), (scale_hbm, scale_ref))
        )
    ]
    barrier = pltpu.get_barrier_semaphore()

    def greet(other):
        pl.semaphore_signal(
            barrier, inc=1, device_id={"seq": other}, device_id_type=pl.DeviceIdType.MESH
        )

    for other in partners:
        greet(other)
    pl.when(pair < pairs - 1)(lambda: greet(above))
    pl.when(pair > 0)(lambda: greet(below))
    pl.semaphore_wait(barrier, len(partners) + jnp.where((pair > 0) & (pair < pairs - 1), 2, 1))

    def for_each_far(turn, action):
        if serve:
            for part in range(2):
                for bit in reversed(range(1, levels)):
                    less = withheld(bit, turn)
                    pl.when(jnp.logical_not(less))(lambda: action(block_copy(bit, turn, part, side)))
                    pl.when(less)(lambda: action(block_copy(bit, turn, part, side, per_chunk - 1)))
            return
        for part in range(2):
            for bit in range(1, levels):
                action(block_copy(bit, turn, part, side))

    def send_far(turn):
        for_each_far(turn, lambda copy: copy.start())

    def send_near(turn, _):
        for part in range(2):
            block_copy(0, turn * step_count, part, 1 - side, per_chunk * step_count).start()
        return 0

    def sent_by(turn):
        more = jnp.maximum(turn - delay(pair) - calm, 0)
        return jnp.minimum(window + turn + 1 + more, chunks)

    if serve:
        @pl.when(lax.rem(pair, 2) == 1)
        def _():
            for index in range(serve):
                ask_copy(index).start()

    lax.fori_loop(0, sent_by(-1), lambda turn, _: (send_far(turn), 0)[1], 0)
    for load in loads:
        load.start()
    lax.fori_loop(0, chunks // step_count, send_near, 0)

    row_ids = lax.broadcasted_iota(jnp.int32, (rows, rows), 0)
    column_ids = lax.broadcasted_iota(jnp.int32, (rows, rows), 1)
    live_rows = lax.broadcasted_iota(jnp.int32, (rows, width), 0)
    root = 1.0 / math.sqrt(width)

    for load in loads:
        load.wait()
    lengths = [len_ref[me]] + [len_ref[partner] for partner in partners]

    def key_value_sum(keys, values, length):
        mapped = jnp.where(live_rows < length, feature(keys.astype(jnp.float32)), 0.0)
        return sum(
            lax.dot_general(
                term, values, (((0,), (0,)), ((), ())), preferred_element_type=jnp.float32
            )
            for term in two_terms(mapped)
        )

    def piece(queries, keys, values, length, causal):
        weights, peak, total = weigh(queries, keys, length, causal)
        return jnp.dot(weights, values, preferred_element_type=jnp.float32), peak, total

    def weigh(queries, keys, length, causal):
        scores = root * lax.dot_general(
            queries, keys, (((1,), (1,)), ((), ())), preferred_element_type=jnp.float32
        )
        allowed = column_ids < length
        if causal:
            allowed = allowed & (column_ids <= row_ids)
        peak = jnp.max(jnp.where(allowed, scores, -jnp.inf), axis=1, keepdims=True)
        weights = jnp.where(allowed, jnp.exp(scores - peak), 0.0).astype(jnp.bfloat16)
        total = jnp.sum(weights.astype(jnp.float32), axis=1, keepdims=True)
        return weights, peak, total

    def merge(pieces):
        top = functools.reduce(jnp.maximum, [peak for _, peak, _ in pieces])
        numerator, denominator = 0.0, 0.0
        for part, peak, total in pieces:
            factor = jnp.exp(peak - top)
            numerator = numerator + factor * part
            denominator = denominator + factor * total
        return numerator / denominator

    def attend(turn, finishing, asked):
        chunk = place(turn, side)
        cuts = [head_columns(chunk * per_chunk + offset) for offset in range(per_chunk)]
        pieces = [
            [
                piece(q_ref[:, cut], k_ref[:, cut], v_ref[:, cut], lengths[0], True),
                piece(q_ref[:, cut], far[0, 0, :, cut], far[0, 1, :, cut], lengths[1], False),
            ]
            for cut in cuts
        ]
        if asked:
            full, cut_short = jnp.where(pair == 1, 2, 1), jnp.where(pair == 1, 1, 2)
            sources = [
                (full, jnp.where(pair == 1, lengths[3], lengths[2]), per_chunk),
                (cut_short, jnp.where(pair == 1, lengths[2], lengths[3]), per_chunk - 1),
            ]
            index = served_index(turn)
            for copy in answer_copies(index):
                copy.wait_recv()
            columns_of = jnp.tile(stats_in[index], (rows // 8, 1)).T
            pieces[-1].append((served_in[index].astype(jnp.float32), columns_of[:, :1], columns_of[:, 1:2]))
        else:
            sources = [(bit, lengths[1 + bit], per_chunk) for bit in range(1, levels)]
        if finishing:
            heavy = []
            for bit, extent, count in sources:
                block_copy(bit, turn, 0, side, count).wait_recv()
                heavy.append([weigh(q_ref[:, cut], far[bit, 0, :, cut], extent, False) for cut in cuts[:count]])
            for (bit, extent, count), weighed in zip(sources, heavy):
                block_copy(bit, turn, 1, side, count).wait_recv()
                for cut, found, (weights, peak, total) in zip(cuts, pieces, weighed):
                    numerator = jnp.dot(weights, far[bit, 1, :, cut], preferred_element_type=jnp.float32)
                    found.append((numerator, peak, total))
        else:
            for bit, extent, count in sources:
                far_arrival(bit, turn, count).wait_recv()
                for cut, found in list(zip(cuts, pieces))[:count]:
                    found.append(piece(q_ref[:, cut], far[bit, 0, :, cut], far[bit, 1, :, cut], extent, False))
        for cut, found in zip(cuts, pieces):
            attention = merge(found)
            if finishing:
                out_ref[:, cut] = (attention + acc[:, cut]).astype(out_ref.dtype)
            else:
                acc[:, cut] = attention

    def answer(index):
        @pl.when(index == 0)
        def _():
            arrival(guest_q, ask_recv.at[0]).wait_recv()

        cut = head_columns((place(served_turn(index), side) + 1) * per_chunk - 1)
        numerator, peak, total = piece(guest_q[index], k_ref[:, cut], v_ref[:, cut], lengths[0], False)
        served_out[index] = numerator.astype(jnp.bfloat16)
        lanes = jnp.where(column_ids == 0, peak, total)
        stats_out[index] = lanes.T[:8]
        for copy in answer_copies(index):
            copy.start()

    def add_linear(head, prefix, finishing):
        cut = head_columns(head)
        near = jnp.where(side > 0, near_sums[head], 0.0)
        prefix = jnp.where(pair > 0, prefix.astype(jnp.float32), 0.0) + near
        coarse, fine = two_terms(feature(q_ref[:, cut].astype(jnp.float32)))
        sums, rest = two_terms(prefix)
        linear = sum(
            jnp.dot(left, right, preferred_element_type=jnp.float32)
            for left, right in ((coarse, sums), (fine, sums), (coarse, rest))
        )
        gain = scale_ref[head] / (width * math.sqrt(rows * blocks))
        linear = gain * linear
        if finishing:
            out_ref[:, cut] = (acc[:, cut] + linear).astype(out_ref.dtype)
        else:
            acc[:, cut] = linear

    def prepare(step):
        chunk = place(step, side)

        @pl.when((step < half) | (side > 0))
        def _():
            for offset in range(per_chunk):
                head = chunk * per_chunk + offset
                cut = head_columns(head)
                near_sums[head] = key_value_sum(far[0, 0, :, cut], far[0, 1, :, cut], lengths[1])

        @pl.when((step < half) & (pair < pairs - 1))
        def _():
            for offset in range(per_chunk):
                cut = head_columns(chunk * per_chunk + offset)
                own_sums[step * per_chunk + offset] = key_value_sum(k_ref[:, cut], v_ref[:, cut], lengths[0])

    def prepare_group(group):
        near_arrival(group).wait_recv()
        for offset in range(step_count):
            prepare(group * step_count + offset)

    def pass_on(number):
        @pl.when(pair > 0)
        def _():
            chain_copy(number).wait_recv()

        @pl.when(pair < pairs - 1)
        def _():
            for part in range(step_count):
                link = number * step_count + part
                first = place(link, side) * per_chunk
                for offset in range(per_chunk):
                    both = own_sums[link * per_chunk + offset] + near_sums[first + offset]
                    before = jnp.where(pair > 0, chain_in[link, offset].astype(jnp.float32), 0.0)
                    chain_out[link, offset] = (both + before).astype(jnp.bfloat16)
            chain_copy(number).start()

        @pl.when(pair > 0)
        def _():
            swap_copy(number).start()

    def linear_round(number):
        @pl.when(pair > 0)
        def _():
            swap_copy(number).wait_recv()

        for part in range(step_count):
            finish_linear(number * step_count + part)

    def finish_linear(late):
        for offset in range(per_chunk):
            add_linear(place(late, side) * per_chunk + offset, chain_in[late, offset], True)

        def other(finishing):
            for offset in range(per_chunk):
                add_linear(place(late, 1 - side) * per_chunk + offset, swap_in[late, offset], finishing)

        if joined:
            pl.when(late < half - 1)(lambda: other(True))
            pl.when(late == half - 1)(lambda: other(False))
        else:
            other(True)

    def one_turn(turn, _):
        pl.when(turn < chunks // step_count)(lambda: prepare_group(turn))
        number = turn - delay(pair)
        pl.when((number >= 0) & (number < rounds))(lambda: pass_on(number))
        lax.fori_loop(sent_by(turn - 1), sent_by(turn), lambda chunk, _: (send_far(chunk), 0)[1], 0)
        pl.when((turn >= linear_lag) & (turn - linear_lag < rounds))(lambda: linear_round(turn - linear_lag))

        if serve:
            @pl.when((pair < pairs // 2) & (turn > 0) & (turn <= serve))
            def _():
                answer(turn - 1)

        asking = served(turn) & (lax.rem(pair, 2) == 1)
        inside = turn < (chunks - 1 if joined else chunks)
        if serve:
            pl.when(inside & jnp.logical_not(asking))(lambda: attend(turn, False, False))
            pl.when(inside & asking)(lambda: attend(turn, False, True))
        else:
            pl.when(inside)(lambda: attend(turn, False, False))
        if joined:
            last = turn == chunks - 1
            if serve:
                pl.when(last & jnp.logical_not(asking))(lambda: attend(turn, True, False))
                pl.when(last & asking)(lambda: attend(turn, True, True))
            else:
                pl.when(last)(lambda: attend(turn, True, False))

        return 0

    @pl.when(pair == 0)
    def _():
        def clear(turn, _):
            chain_in[turn] = jnp.zeros_like(chain_in[turn])
            swap_in[turn] = jnp.zeros_like(swap_in[turn])
            return 0

        lax.fori_loop(0, half, clear, 0)

    lax.fori_loop(0, turns, one_turn, 0)

    for part, source in enumerate((k_hbm, v_hbm)):
        departure(source, send_sem.at[0, part]).wait_send()
        for bit in range(1, levels):
            if serve:
                pl.when(pair != bit - 1)(departure(source, send_sem.at[bit, part]).wait_send)
                some = source.at[:, :(heads - serve) * width]
                pl.when(pair == bit - 1)(departure(some, send_sem.at[bit, part]).wait_send)
            else:
                departure(source, send_sem.at[bit, part]).wait_send()

    pl.when(pair < pairs - 1)(departure(chain_out, chain_send.at[0]).wait_send)
    pl.when(pair > 0)(departure(chain_in, swap_send.at[0]).wait_send)

    if serve:
        @pl.when(lax.rem(pair, 2) == 1)
        def _():
            departure(guest_q, ask_send.at[0]).wait_send()

        @pl.when(pair < pairs // 2)
        def _():
            departure(served_out, answer_send.at[0]).wait_send()
            departure(stats_out, answer_send.at[1]).wait_send()


def delay(pair):
    return (LAG_TIMES * pair + 1) // LAG_OVER


def shards(blocks, query_rows, key_rows, value_rows, key_len, linear_scale):
    rows, total = query_rows.shape
    heads = linear_scale.shape[0]
    width = total // heads
    levels = blocks.bit_length() - 1
    chunks = heads // HEADS_PER_CHUNK
    half = chunks // 2
    step_count = STEPS if half % STEPS == 0 else 1
    serve = SERVED if blocks == 8 else 0
    guests = max(serve, 1)
    vmem = pl.BlockSpec(memory_space=pltpu.VMEM)
    hbm = pl.BlockSpec(memory_space=pltpu.HBM)
    piece = (half, HEADS_PER_CHUNK, width, width)
    dma = pltpu.SemaphoreType.DMA
    return pl.pallas_call(
        functools.partial(kernel, blocks, heads, width, HEADS_PER_CHUNK, WINDOW, CALM, delay, serve),
        out_shape=jax.ShapeDtypeStruct((rows, total), query_rows.dtype),
        in_specs=[hbm, hbm, hbm, hbm, hbm],
        out_specs=vmem,
        scratch_shapes=[
            pltpu.SMEM((blocks,), jnp.int32),
            pltpu.SMEM((heads,), jnp.float32),
            pltpu.VMEM((rows, total), jnp.bfloat16),
            pltpu.VMEM((rows, total), jnp.bfloat16),
            pltpu.VMEM((rows, total), jnp.bfloat16),
            dma((5,)),
            pltpu.VMEM((levels, 2, rows, total), jnp.bfloat16),
            pltpu.VMEM((rows, total), jnp.float32),
            pltpu.VMEM((heads // 2, width, width), jnp.float32),
            pltpu.VMEM((heads, width, width), jnp.float32),
            pltpu.VMEM(piece, jnp.bfloat16),
            pltpu.VMEM(piece, jnp.bfloat16),
            pltpu.VMEM(piece, jnp.bfloat16),
            dma((levels, 2)),
            dma((levels - 1, chunks + 1)),
            dma((chunks // step_count,)),
            dma((1,)),
            dma((half // step_count,)),
            dma((1,)),
            dma((half // step_count,)),
            pltpu.VMEM((guests, rows, width), jnp.bfloat16),
            pltpu.VMEM((guests, rows, width), jnp.bfloat16),
            pltpu.VMEM((guests, rows, width), jnp.bfloat16),
            pltpu.VMEM((guests, 8, rows), jnp.float32),
            pltpu.VMEM((guests, 8, rows), jnp.float32),
            dma((1,)),
            dma((1,)),
            dma((2,)),
            dma((guests, 2)),
        ],
        compiler_params=pltpu.CompilerParams(
            collective_id=0, has_side_effects=True, vmem_limit_bytes=55000000
        ),
        name="butterfly",
    )(
        pltpu.with_memory_space_constraint(key_len, pltpu.HBM),
        pltpu.with_memory_space_constraint(linear_scale, pltpu.HBM),
        query_rows, key_rows, value_rows,
    )


def solution(mesh):
    return jax.shard_map(
        functools.partial(shards, mesh.shape["seq"]),
        mesh=mesh,
        in_specs=(
            P(("groups", "seq"), "head"),
            P(("groups", "seq"), "head"),
            P(("groups", "seq"), "head"),
            P("groups"),
            P("head"),
        ),
        out_specs=P(("groups", "seq"), "head"),
        check_vma=False,
    )
```
